256 devices in a mesh: section: 8 (over y, x_lo), dp: 32 (over x_hi, z, core).
Axes of the slice: x: 4 (x_hi: 2, x_lo: 2; x = x_hi * 2 + x_lo), y: 4, z: 8, core: 2. Of those that a mesh axis runs over, the one named last changes fastest.
Arguments:
- images: bfloat16 [4, 6144, 512], P(None, 'dp'), may hold values from -6 to 6
- out_grad: bfloat16 [4, 6144, 512], P(None, 'dp'), may hold values from -0.0390625 to 0.0390625
- w_in: bfloat16 [8, 2, 512, 512], P('section'), may hold values from -0.25 to 0.25
- w_out: bfloat16 [8, 2, 512, 512], P('section'), may hold values from -0.25 to 0.25
Outputs:
- grad_in: float32 [8, 2, 512, 512], P('section', None, 'dp')
- grad_out: float32 [8, 2, 512, 512], P('section', None, 'dp')
The draws below stay inside these ranges and needn't reach their ends.
All inputs are finite; a program needn't handle non-finite values.
Results may differ from the reference program's by a relative error of at most 0.04.
Values may be sent and summed in bfloat16 or wider, within the bound.
A program may use at most 64 MiB of HBM per device.

```python
import jax
import jax.numpy as jnp
from jax import lax

C = 512
MICRO = 4
CELLS = 2
SECTIONS = 8
ROWS = 6144


def levels(key, extent, pieces, least, high):
    def one(dim, shards_of):
        steps = jax.random.uniform(jax.random.fold_in(jax.random.fold_in(key, 6), dim), (shards_of,), jnp.float32, least / len(pieces), high / len(pieces))
        return jnp.repeat(jnp.exp(steps), extent[dim] // shards_of).reshape((-1,) + (1,) * (len(extent) - dim - 1))

    factor_of = one(*pieces[0])
    for cut in pieces[1:]:
        factor_of = factor_of * one(*cut)
    return factor_of


def gaussian(rng, shape, spread, most, split=(), held_as=jnp.bfloat16):
    array = jax.random.normal(rng, shape, jnp.float32) * spread
    if len(split) > 0:
        array = levels(rng, shape, split, -0.22, 0.18) * array
    return jnp.clip(array, min=-most, max=most).astype(held_as)


def setup_inputs(seed: int = 0) -> dict:
    key_of = jax.random.split(jax.random.key(seed), 5)
    return {
        "images": gaussian(key_of[0], (MICRO, ROWS, C), 1.0, 6.0, ((1, 32),)),
        "out_grad": gaussian(key_of[1], (MICRO, ROWS, C), (1.0 / (MICRO * ROWS) ** 0.5), 0.0390625, ((1, 32),)),
        "w_in": gaussian(key_of[2], (SECTIONS, CELLS, C, C), C ** -0.5, 0.25, ((0, 8),)),
        "w_out": gaussian(key_of[3], (SECTIONS, CELLS, C, C), C ** -0.5, 0.25, ((0, 8),)),
    }


norm_epsilon = 1e-06

def norm_scale(values):
    return lax.rsqrt(lax.optimization_barrier(jnp.mean(values * values, axis=-1, keepdims=True)) + norm_epsilon)

def cell_forward(current, weight_in, weight_out):
    wide = current.astype(jnp.float32)
    scale = norm_scale(wide)
    normed = (wide * scale).astype(jnp.bfloat16)
    pre_act = jnp.dot(normed, weight_in, preferred_element_type=jnp.float32)
    hidden = jax.nn.silu(pre_act).astype(jnp.bfloat16)
    result = (wide + jnp.dot(hidden, weight_out, preferred_element_type=jnp.float32)).astype(jnp.bfloat16)
    return (result, (normed, pre_act, hidden))

def cell_backward(grad_y, current, retained, weight_in, weight_out):
    normed, pre_act, hidden = retained
    grad_wout = jnp.dot(hidden.T, grad_y, preferred_element_type=jnp.float32)
    grad_hidden = jnp.dot(grad_y, weight_out.T, preferred_element_type=jnp.float32)
    sigmoid_act = jax.nn.sigmoid(pre_act)
    grad_pre = (grad_hidden * sigmoid_act * (1.0 + pre_act * (1.0 - sigmoid_act))).astype(jnp.bfloat16)
    grad_win = jnp.dot(normed.T, grad_pre, preferred_element_type=jnp.float32)
    grad_normed = jnp.dot(grad_pre, weight_in.T, preferred_element_type=jnp.float32)
    wide = current.astype(jnp.float32)
    scale = norm_scale(wide)
    grad_wide = scale * (grad_normed - wide * scale * scale * lax.optimization_barrier(jnp.mean(grad_normed * wide, axis=-1, keepdims=True)))
    return ((grad_y.astype(jnp.float32) + grad_wide).astype(jnp.bfloat16), grad_win, grad_wout)

def reference(images, out_grad, w_in, w_out):
    section_count = w_in.shape[0]
    cell_count = w_in.shape[1]
    total_in = jnp.zeros(w_in.shape, jnp.float32)
    total_out = jnp.zeros(w_out.shape, jnp.float32)
    for micro_index in range(images.shape[0]):
        current = images[micro_index]
        history = []
        for section_index in range(section_count):
            for cell_index in range(cell_count):
                result, retained = cell_forward(current, w_in[section_index, cell_index], w_out[section_index, cell_index])
                history.append((section_index, cell_index, current, retained))
                current = result
        grad_y = out_grad[micro_index]
        for section_index, cell_index, current, retained in reversed(history):
            grad_y, grad_win, grad_wout = cell_backward(grad_y, current, retained, w_in[section_index, cell_index], w_out[section_index, cell_index])
            total_in = total_in.at[section_index, cell_index].add(grad_win)
            total_out = total_out.at[section_index, cell_index].add(grad_wout)
    return (total_in, total_out)
```

```python
import jax
import jax.numpy as jnp
from jax import lax
from jax.experimental import pallas as pl
from jax.experimental.pallas import tpu as pltpu
from jax.sharding import PartitionSpec as P

norm_epsilon = 1e-06
f32, bf16 = jnp.float32, jnp.bfloat16
MESH = pl.DeviceIdType.MESH
C = 512
M = 4
R = 96
DMA = pltpu.SemaphoreType.DMA


def dot(a, b):
    return jnp.dot(a, b, preferred_element_type=f32)


def dot_bt(a, b):
    return lax.dot_general(a, b, (((1,), (1,)), ((), ())), preferred_element_type=f32)


def dot_at(a, b):
    return lax.dot_general(a, b, (((0,), (0,)), ((), ())), preferred_element_type=f32)


def kernel(
    img, og, wi, wo, gi_out, go_out,
    WI, WO, X, N, H, GP, GY, D, PRE, RS, G, RC, S, L1, L2, T, LZ,
    loc_w, loc_m, ag_s, ag_r, fw_s, fw_r, f_s, f_r, b_s, b_r, c_s, c_r, p_s, p_r, q_s, q_r, z_s, z_r,
):
    sec = lax.axis_index("section")
    dp = lax.axis_index("dp")
    y, xl = sec // 2, sec % 2
    xh, z, c = dp // 16, (dp // 2) % 8, dp % 2
    x = xh * 2 + xl

    def dev(x_, y_, z_, c_):
        return (y_ * 2 + x_ % 2, (x_ // 2) * 16 + z_ * 2 + c_)

    right, left = dev((x + 1) % 4, y, z, c), dev((x + 3) % 4, y, z, c)
    up, down = dev(x, (y + 1) % 4, z, c), dev(x, (y + 3) % 4, z, c)
    sib = dev(x, y, z, 1 - c)

    def ring_z(off):
        return dev(x, y, (z + off) % 8, c)

    def rc(src, dst, ss, rs, to):
        return pltpu.make_async_remote_copy(
            src_ref=src, dst_ref=dst, send_sem=ss, recv_sem=rs, device_id=to, device_id_type=MESH
        )

    mine, other = 2 * xl, 2 * (1 - xl)

    def load_w(i):
        src, dst = ((wi, WI), (wo, WO))[i]
        return pltpu.make_async_copy(src.at[0], dst.at[pl.ds(mine, 2)], loc_w.at[i])

    def load_img(m):
        return pltpu.make_async_copy(img.at[m, pl.ds(xl * R, R)], X.at[0, m], loc_m.at[m])

    def load_og(m):
        return pltpu.make_async_copy(og.at[m, pl.ds(xl * R, R)], GY.at[4, m], loc_m.at[m])

    load_w(0).start()
    load_w(1).start()

    @pl.when(y == 0)
    def _():
        for m in range(M):
            load_img(m).start()

    @pl.when(y == 3)
    def _():
        for m in range(M):
            load_og(m).start()

    bar = pltpu.get_barrier_semaphore()
    peers = [right, left, up, down, sib] + [ring_z(o) for o in range(1, 8)]
    for to in peers:
        pl.semaphore_signal(bar, inc=1, device_id=to, device_id_type=MESH)
    pl.semaphore_wait(bar, len(peers))

    def ag(t, side):
        src, dst = ((wi, WI), (wo, WO))[t % 2]
        k = t // 2
        rows = pl.ds(c * 256 + side * 128, 128)
        return rc(src.at[0, k, rows], dst.at[mine + k, rows], ag_s.at[t, side], ag_r.at[t, side], (right, left)[side])

    def fw(t):
        dst = (WI, WO)[t % 2]
        here = dst.at[other + t // 2, pl.ds(c * 256, 256)]
        return rc(here, here, fw_s.at[t], fw_r.at[t], sib)

    for t in range(4):
        for side in range(2):
            ag(t, side).start()
    for t in range(4):
        for side in range(2):
            ag(t, side).wait_recv()
        fw(t).start()
    load_w(0).wait()
    load_w(1).wait()
    for t in range(4):
        fw(t).wait_recv()

    def f_send(m):
        return rc(X.at[4, m], X.at[0, m], f_s.at[m], f_r.at[m], up)

    def forward(m, carry):
        @pl.when(y == 0)
        def _():
            load_img(m).wait()

        @pl.when(y > 0)
        def _():
            f_send(m).wait_recv()

        for j in range(4):
            xb = X[j, m]
            wide = xb.astype(f32)
            r = lax.rsqrt(jnp.mean(wide * wide, axis=-1, keepdims=True) + norm_epsilon)
            RS[j, m] = jnp.broadcast_to(r, (R, 128))
            N[j, m] = (wide * r).astype(bf16)
            p = dot(xb, WI[j]) * r
            PRE[j, m] = p
            s = 1.0 / (1.0 + jnp.exp(-p))
            h = p * s
            D[j, m] = s + h * (1.0 - s)
            hb = h.astype(bf16)
            H[j, m] = hb
            X[j + 1, m] = (wide + dot(hb, WO[j])).astype(bf16)

        @pl.when(y < 3)
        def _():
            f_send(m).start()

        return carry

    lax.fori_loop(0, M, forward, 0)

    def b_send(m):
        return rc(GY.at[0, m], GY.at[4, m], b_s.at[m], b_r.at[m], down)

    def backward(m, carry):
        @pl.when(y == 3)
        def _():
            load_og(m).wait()

        @pl.when(y < 3)
        def _():
            b_send(m).wait_recv()

        for j in range(3, -1, -1):
            gy = GY[j + 1, m]
            gp = (dot_bt(gy, WO[j]) * D[j, m]).astype(bf16)
            GP[j, m] = gp
            q = jnp.sum(gp.astype(f32) * PRE[j, m], axis=-1, keepdims=True) * (1.0 / C)
            gn = dot_bt(gp, WI[j])
            r = RS[j, m][:, :1]
            GY[j, m] = (gy.astype(f32) + r * (gn - N[j, m].astype(f32) * q)).astype(bf16)

        @pl.when(y > 0)
        def _():
            b_send(m).start()

        return carry

    lax.fori_loop(0, M, backward, 0)

    def cell_at(t):
        return lax.select(t < 2, mine + 1 - t, other + 3 - t)

    def c_send(t):
        j = cell_at(t)
        return rc(G.at[j, :, :, :, 1 - c], RC.at[j], c_s.at[t], c_r.at[t], sib)

    def weight(t, carry):
        j = cell_at(t)
        gi = dot_at(N[j].reshape(M * R, C), GP[j].reshape(M * R, C))
        G[j, 0] = gi.astype(bf16).reshape(2, 8, 2, 16, C)
        go = dot_at(H[j].reshape(M * R, C), GY[j + 1].reshape(M * R, C))
        G[j, 1] = go.astype(bf16).reshape(2, 8, 2, 16, C)
        c_send(t).start()
        return carry

    lax.fori_loop(0, 4, weight, 0)

    xh_r, xh_l = ((x + 1) % 4) // 2, ((x + 3) % 4) // 2

    def l1(k, side):
        return rc(
            S.at[mine + k, :, 1 - xh, pl.ds(side * 4, 4)], L1.at[k, side],
            p_s.at[k, side], p_r.at[k, side], (right, left)[side],
        )

    def l2(k, side, half):
        return rc(
            S.at[other + k, :, (xh_r, xh_l)[side], pl.ds(half * 4, 4)], L2.at[k, side, :, pl.ds(half * 4, 4)],
            q_s.at[k, side, half], q_r.at[k, side, half], (right, left)[side],
        )

    def sibling_sum(t):
        j = cell_at(t)
        c_send(t).wait_recv()
        S[j] = (G[j, :, :, :, c].astype(f32) + RC[j].astype(f32)).astype(bf16)

    def own_out(t, carry):
        sibling_sum(t)
        k = 1 - t
        l1(k, 0).start()
        l1(k, 1).start()
        return carry

    def other_out(t, carry):
        sibling_sum(t)
        k = 3 - t
        l2(k, 0, 1).start()
        l2(k, 1, 0).start()
        return carry

    lax.fori_loop(0, 2, own_out, 0)
    lax.fori_loop(2, 4, other_out, 0)

    def relay(t, carry):
        k = 1 - t
        for side, xd in ((0, xh_r), (1, xh_l)):
            l1(k, side).wait_recv()
            rows = pl.ds(side * 4, 4)
            S[other + k, :, xd, rows] = (
                S[other + k, :, xd, rows].astype(f32) + L1[k, side].astype(f32)
            ).astype(bf16)
            l2(k, side, side).start()
        return carry

    lax.fori_loop(0, 2, relay, 0)

    def z_send(k, off):
        return rc(T.at[k, :, (z + off) % 8], LZ.at[k, off - 1], z_s.at[k, off - 1], z_r.at[k, off - 1], ring_z(off))

    def collect(t, carry):
        k = 1 - t
        for side in range(2):
            for half in range(2):
                l2(k, side, half).wait_recv()
        T[k] = (S[mine + k, :, xh].astype(f32) + L2[k, 0].astype(f32) + L2[k, 1].astype(f32)).astype(bf16)
        for off in (4, 3, 5, 2, 6, 1, 7):
            z_send(k, off).start()
        return carry

    lax.fori_loop(0, 2, collect, 0)

    def finish(t, carry):
        k = 1 - t
        total = T[k, :, z].astype(f32)
        for off in range(1, 8):
            z_send(k, off).wait_recv()
            total = total + LZ[k, off - 1].astype(f32)
        gi_out[k] = total[0]
        go_out[k] = total[1]
        return carry

    lax.fori_loop(0, 2, finish, 0)

    for t in range(4):
        for side in range(2):
            ag(t, side).wait_send()
        fw(t).wait_send()
        c_send(jnp.int32(t)).wait_send()

    @pl.when(y < 3)
    def _():
        for m in range(M):
            f_send(m).wait_send()

    @pl.when(y > 0)
    def _():
        for m in range(M):
            b_send(m).wait_send()

    for k in range(2):
        for side in range(2):
            l1(k, side).wait_send()
            for half in range(2):
                l2(k, side, half).wait_send()
        for off in range(1, 8):
            z_send(k, off).wait_send()


def local(images, out_grad, w_in, w_out):
    V = pltpu.VMEM
    scratch = [
        V((4, C, C), bf16), V((4, C, C), bf16),
        V((5, M, R, C), bf16), V((4, M, R, C), bf16), V((4, M, R, C), bf16), V((4, M, R, C), bf16),
        V((5, M, R, C), bf16), V((4, M, R, C), f32), V((4, M, R, C), f32), V((4, M, R, 128), f32),
        V((4, 2, 2, 8, 2, 16, C), bf16), V((4, 2, 2, 8, 16, C), bf16), V((4, 2, 2, 8, 16, C), bf16),
        V((2, 2, 2, 4, 16, C), bf16), V((2, 2, 2, 8, 16, C), bf16), V((2, 2, 8, 16, C), bf16),
        V((2, 7, 2, 16, C), bf16),
        DMA((2,)), DMA((M,)), DMA((4, 2)), DMA((4, 2)), DMA((4,)), DMA((4,)),
        DMA((M,)), DMA((M,)), DMA((M,)), DMA((M,)), DMA((4,)), DMA((4,)),
        DMA((2, 2)), DMA((2, 2)), DMA((2, 2, 2)), DMA((2, 2, 2)), DMA((2, 7)), DMA((2, 7)),
    ]
    out = jax.ShapeDtypeStruct((2, 16, C), f32)
    grad_in, grad_out = pl.pallas_call(
        kernel,
        out_shape=(out, out),
        in_specs=[pl.BlockSpec(memory_space=pl.ANY)] * 4,
        out_specs=(pl.BlockSpec(memory_space=pltpu.VMEM),) * 2,
        scratch_shapes=scratch,
        compiler_params=pltpu.CompilerParams(
            collective_id=0, has_side_effects=True, vmem_limit_bytes=60 * 2**20
        ),
        name="window",
    )(images, out_grad, w_in, w_out)
    return grad_in[None], grad_out[None]


def solution(mesh):
    return jax.shard_map(
        local,
        mesh=mesh,
        in_specs=(
            P(None, "dp", None),
            P(None, "dp", None),
            P("section", None, None, None),
            P("section", None, None, None),
        ),
        out_specs=(P("section", None, "dp", None), P("section", None, "dp", None)),
        check_vma=False,
    )
```

```python
import jax
import jax.numpy as jnp
from jax import lax
from jax.experimental import pallas as pl
from jax.experimental.pallas import tpu as pltpu
from jax.sharding import PartitionSpec as P

norm_epsilon = 1e-06
f32, bf16 = jnp.float32, jnp.bfloat16
MESH = pl.DeviceIdType.MESH
C = 512
M = 4
R = 96
DMA = pltpu.SemaphoreType.DMA


def dot(a, b):
    return jnp.dot(a, b, preferred_element_type=f32)


def dot_at(a, b):
    return lax.dot_general(a, b, (((0,), (0,)), ((), ())), preferred_element_type=f32)


def kernel(
    img, og, wi, wo, gi_out, go_out,
    WI, WO, WIT, WOT, X, XT, XO, N, H, GP, GY, D, PRE, RS, G, RC, S, L1, L2, T, LZ,
    loc_w, loc_m, loc_x, ag_s, ag_r, fw_s, fw_r, g_s, g_r, f_s, f_r, b_s, b_r, c_s, c_r, p_s, p_r, q_s, q_r, z_s, z_r,
    near_z, diag,
):
    sec = lax.axis_index("section")
    dp = lax.axis_index("dp")
    y, xl = sec // 2, sec % 2
    xh, z, c = dp // 16, (dp // 2) % 8, dp % 2
    x = xh * 2 + xl

    def dev(x_, y_, z_, c_):
        return (y_ * 2 + x_ % 2, (x_ // 2) * 16 + z_ * 2 + c_)

    right, left = dev((x + 1) % 4, y, z, c), dev((x + 3) % 4, y, z, c)
    up, down = dev(x, (y + 1) % 4, z, c), dev(x, (y + 3) % 4, z, c)
    up_right = dev((x + 1) % 4, (y + 1) % 4, z, c)
    sib = dev(x, y, z, 1 - c)

    def ring_z(off):
        return dev(x, y, (z + off) % 8, c)

    def rc(src, dst, ss, rs, to):
        return pltpu.make_async_remote_copy(
            src_ref=src, dst_ref=dst, send_sem=ss, recv_sem=rs, device_id=to, device_id_type=MESH
        )

    def signal(sem, to):
        pl.semaphore_signal(sem, inc=1, device_id=to, device_id_type=MESH)

    mine, other = 2 * xl, 2 * (1 - xl)

    def load_w(i):
        src, dst = ((wi, WI), (wo, WO))[i]
        return pltpu.make_async_copy(src.at[0], dst.at[pl.ds(mine, 2)], loc_w.at[i])

    def load_img(m):
        return pltpu.make_async_copy(img.at[m, pl.ds(xl * R, R)], X.at[0, m], loc_m.at[m])

    def load_partner_img(m):
        return pltpu.make_async_copy(img.at[m, pl.ds(R, R)], XT.at[m], loc_x.at[m])

    def load_og(m):
        return pltpu.make_async_copy(og.at[m, pl.ds(xl * R, R)], GY.at[4, m], loc_m.at[m])

    load_w(0).start()
    load_w(1).start()

    @pl.when(y == 0)
    def _():
        for m in range(M):
            load_img(m).start()

            @pl.when(xl == 0)
            def _():
                load_partner_img(m).start()

    @pl.when(y == 3)
    def _():
        for m in range(M):
            load_og(m).start()

    bar = pltpu.get_barrier_semaphore()
    peers = [right, left, up, down, sib, ring_z(1), ring_z(7)]
    for to in peers:
        signal(bar, to)
    pl.semaphore_wait(bar, len(peers))

    def z_round(n):
        for off in (1, 7):
            signal(near_z.at[n], ring_z(off))

    z_round(0)

    @pl.when((y == 1) & (xl == 1))
    def _():
        signal(diag, down)

    def ag(t, side):
        src, dst = ((wi, WI), (wo, WO))[t % 2]
        k = t // 2
        rows = pl.ds(c * 256 + side * 128, 128)
        return rc(src.at[0, k, rows], dst.at[mine + k, rows], ag_s.at[t, side], ag_r.at[t, side], (right, left)[side])

    def ag_start():
        for t in range(4):
            for side in range(2):
                ag(t, side).start()

    def fw(t):
        dst = (WI, WO)[t % 2]
        here = dst.at[other + t // 2, pl.ds(c * 256, 256)]
        return rc(here, here, fw_s.at[t], fw_r.at[t], sib)

    def ag_forward():
        for t in range(4):
            for side in range(2):
                ag(t, side).wait_recv()
            fw(t).start()

    def fw_wait():
        for t in range(4):
            fw(t).wait_recv()

    def transpose_weights():
        def one(j, carry):
            WIT[j] = WI[j].T
            WOT[j] = WO[j].T
            return carry

        lax.fori_loop(0, 4, one, 0)

    def cell(xb, j, m, save=True, finish=True):
        wide = xb.astype(f32)
        r = lax.rsqrt(jnp.mean(wide * wide, axis=-1, keepdims=True) + norm_epsilon)
        p = dot(xb, WI[j]) * r
        s = 1.0 / (1.0 + jnp.exp(-p))
        h = p * s
        hb = h.astype(bf16)
        if save:
            RS[j, m] = jnp.broadcast_to(r, (R, 128))
            N[j, m] = (wide * r).astype(bf16)
            PRE[j, m] = p
            D[j, m] = s + h * (1.0 - s)
            H[j, m] = hb
        if finish:
            return (wide + dot(hb, WO[j])).astype(bf16)

    def f_send(m):
        return rc(X.at[4, m], X.at[0, m], f_s.at[m], f_r.at[m], up)

    def to_left(m):
        return rc(X.at[2, m], XT.at[m], g_s.at[m, 0], g_r.at[m, 1], left)

    def to_right(m):
        return rc(XO.at[m], X.at[2, m], g_s.at[m, 1], g_r.at[m, 0], right)

    def to_up(m):
        return rc(X.at[4, m], X.at[0, m], g_s.at[m, 0], f_r.at[m], up)

    def to_up_right(m):
        return rc(XO.at[m], X.at[0, m], g_s.at[m, 1], f_r.at[m], up_right)

    def first_row(m, carry):
        @pl.when(xl == 0)
        def _():
            load_img(m).wait()

        @pl.when(xl == 1)
        def _():
            to_right(m).wait_recv()

        xb = X[mine, m]
        for i in range(2):
            xb = cell(xb, mine + i, m)
            X[mine + i + 1, m] = xb

        @pl.when(xl == 0)
        def _():
            to_left(m).start()
            load_partner_img(m).wait()

        @pl.when(xl == 1)
        def _():
            to_up(m).start()
            to_left(m).wait_recv()

        xb = XT[m]
        for i in range(2):
            xb = cell(xb, mine + i, m, save=False)
        XO[m] = xb

        @pl.when(xl == 0)
        def _():
            to_right(m).start()

        @pl.when(xl == 1)
        def _():
            to_up_right(m).start()

        return carry

    def again(m, carry):
        X[other + 1, m] = cell(X[other, m], other, m)
        cell(X[other + 1, m], other + 1, m, finish=False)
        return carry

    def forward(m, carry):
        f_send(m).wait_recv()
        for j in range(4):
            for i in range(2):
                @pl.when((m == 0) & (y == 1) & (xl != j // 2))
                def _():
                    fw(2 * (j % 2) + i).wait_recv()

            X[j + 1, m] = cell(X[j, m], j, m)

        @pl.when(y < 3)
        def _():
            f_send(m).start()

        return carry

    @pl.when((y > 0) | (xl == 1))
    def _():
        ag_start()

    load_w(0).wait()
    load_w(1).wait()

    @pl.when(y == 0)
    def _():
        @pl.when(xl == 1)
        def _():
            pl.semaphore_wait(diag, 1)

        lax.fori_loop(0, M, first_row, 0)

        @pl.when(xl == 0)
        def _():
            ag_start()

        ag_forward()
        fw_wait()

        @pl.when(xl == 1)
        def _():
            for m in range(M):
                load_img(m).wait()

        lax.fori_loop(0, M, again, 0)

    @pl.when(y > 0)
    def _():
        ag_forward()

        @pl.when(y > 1)
        def _():
            fw_wait()
            transpose_weights()

        lax.fori_loop(0, M, forward, 0)

    @pl.when(y < 2)
    def _():
        transpose_weights()

    pl.semaphore_wait(near_z.at[0], 2)
    z_round(1)

    def b_send(m):
        return rc(GY.at[0, m], GY.at[4, m], b_s.at[m], b_r.at[m], down)

    def backward(m, carry):
        @pl.when(y == 3)
        def _():
            load_og(m).wait()

        @pl.when(y < 3)
        def _():
            b_send(m).wait_recv()

        for j in range(3, -1, -1):
            gy = GY[j + 1, m]
            gp = (dot(gy, WOT[j]) * D[j, m]).astype(bf16)
            GP[j, m] = gp
            q = jnp.sum(gp.astype(f32) * PRE[j, m], axis=-1, keepdims=True) * (1.0 / C)
            gn = dot(gp, WIT[j])
            r = RS[j, m][:, :1]
            GY[j, m] = (gy.astype(f32) + r * (gn - N[j, m].astype(f32) * q)).astype(bf16)

        @pl.when(y > 0)
        def _():
            b_send(m).start()

        return carry

    lax.fori_loop(0, 2, backward, 0)
    pl.semaphore_wait(near_z.at[1], 2)
    z_round(2)
    lax.fori_loop(2, M, backward, 0)

    def c_send(j, io):
        return rc(G.at[j, io, :, :, 1 - c], RC.at[j, io], c_s.at[j, io], c_r.at[j, io], sib)

    def weight(j, io):
        a, b = ((N.at[j], GP.at[j]), (H.at[j], GY.at[j + 1]))[io]
        g = dot_at(a[...].reshape(M * R, C), b[...].reshape(M * R, C))
        G[j, io] = g.astype(bf16).reshape(2, 8, 2, 16, C)
        c_send(j, io).start()

    xh_r, xh_l = ((x + 1) % 4) // 2, ((x + 3) % 4) // 2

    def l1(k, io, side):
        return rc(
            S.at[mine + k, io, 1 - xh, pl.ds(side * 4, 4)], L1.at[k, io, side],
            p_s.at[k, io, side], p_r.at[k, io, side], (right, left)[side],
        )

    def l2(k, io, side, half):
        rows = pl.ds(half * 4, 4)
        return rc(
            S.at[other + k, io, (xh_r, xh_l)[side], rows], L2.at[k, io, side, rows],
            q_s.at[k, io, side, half], q_r.at[k, io, side, half], (right, left)[side],
        )

    def sibling_sum(j, io):
        c_send(j, io).wait_recv()
        S[j, io] = (G[j, io, :, :, c].astype(f32) + RC[j, io].astype(f32)).astype(bf16)

    pieces = [(1, 0), (1, 1), (0, 0), (0, 1)]

    def own_out(k, io):
        sibling_sum(mine + k, io)
        l1(k, io, 0).start()
        l1(k, io, 1).start()

    for k, io in pieces:
        weight(mine + k, io)
    for n in range(4):
        weight(other + pieces[n][0], pieces[n][1])
        own_out(*pieces[n])

    for k, io in pieces:
        sibling_sum(other + k, io)
        l2(k, io, 0, 1).start()
        l2(k, io, 1, 0).start()
        for side, xd in ((0, xh_r), (1, xh_l)):
            l1(k, io, side).wait_recv()
            rows = pl.ds(side * 4, 4)
            S[other + k, io, xd, rows] = (
                S[other + k, io, xd, rows].astype(f32) + L1[k, io, side].astype(f32)
            ).astype(bf16)
            l2(k, io, side, side).start()

    pl.semaphore_wait(near_z.at[2], 2)

    def z_send(k, io, off):
        return rc(
            T.at[k, io, (z + off) % 8], LZ.at[k, io, off - 1],
            z_s.at[k, io, off - 1], z_r.at[k, io, off - 1], ring_z(off),
        )

    for k, io in pieces:
        for side in range(2):
            for half in range(2):
                l2(k, io, side, half).wait_recv()
        T[k, io] = (
            S[mine + k, io, xh].astype(f32) + L2[k, io, 0].astype(f32) + L2[k, io, 1].astype(f32)
        ).astype(bf16)
        for off in (4, 3, 5, 2, 6, 1, 7):
            z_send(k, io, off).start()

    for k, io in pieces:
        total = T[k, io, z].astype(f32)
        for off in range(1, 8):
            z_send(k, io, off).wait_recv()
            total = total + LZ[k, io, off - 1].astype(f32)
        (gi_out, go_out)[io][k] = total

    for t in range(4):
        for side in range(2):
            ag(t, side).wait_send()
        fw(t).wait_send()

    @pl.when(y == 0)
    def _():
        for m in range(M):
            to_left(m).wait_send()
            to_right(m).wait_send()

    @pl.when((y > 0) & (y < 3))
    def _():
        for m in range(M):
            f_send(m).wait_send()

    @pl.when(y > 0)
    def _():
        for m in range(M):
            b_send(m).wait_send()

    for j in range(4):
        for io in range(2):
            c_send(j, io).wait_send()
    for k, io in pieces:
        for side in range(2):
            l1(k, io, side).wait_send()
            for half in range(2):
                l2(k, io, side, half).wait_send()
        for off in range(1, 8):
            z_send(k, io, off).wait_send()


def local(images, out_grad, w_in, w_out):
    V = pltpu.VMEM
    REG = pltpu.SemaphoreType.REGULAR
    weights = V((4, C, C), bf16)
    acts = V((4, M, R, C), bf16)
    wide = V((4, M, R, C), f32)
    scratch = [
        weights, weights, weights, weights,
        V((5, M, R, C), bf16), V((M, R, C), bf16), V((M, R, C), bf16),
        acts, acts, acts, V((5, M, R, C), bf16), wide, wide, V((4, M, R, 128), f32),
        V((4, 2, 2, 8, 2, 16, C), bf16), V((4, 2, 2, 8, 16, C), bf16), V((4, 2, 2, 8, 16, C), bf16),
        V((2, 2, 2, 4, 16, C), bf16), V((2, 2, 2, 8, 16, C), bf16), V((2, 2, 8, 16, C), bf16),
        V((2, 2, 7, 16, C), bf16),
        DMA((2,)), DMA((M,)), DMA((M,)), DMA((4, 2)), DMA((4, 2)), DMA((4,)), DMA((4,)),
        DMA((M, 2)), DMA((M, 2)), DMA((M,)), DMA((M,)), DMA((M,)), DMA((M,)), DMA((4, 2)), DMA((4, 2)),
        DMA((2, 2, 2)), DMA((2, 2, 2)), DMA((2, 2, 2, 2)), DMA((2, 2, 2, 2)), DMA((2, 2, 7)), DMA((2, 2, 7)),
        REG((3,)), REG,
    ]
    out = jax.ShapeDtypeStruct((2, 16, C), f32)
    grad_in, grad_out = pl.pallas_call(
        kernel,
        out_shape=(out, out),
        in_specs=[pl.BlockSpec(memory_space=pl.ANY)] * 4,
        out_specs=(pl.BlockSpec(memory_space=pltpu.VMEM),) * 2,
        scratch_shapes=scratch,
        compiler_params=pltpu.CompilerParams(
            collective_id=0, has_side_effects=True, vmem_limit_bytes=60 * 2**20
        ),
        name="window",
    )(images, out_grad, w_in, w_out)
    return grad_in[None], grad_out[None]


def solution(mesh):
    return jax.shard_map(
        local,
        mesh=mesh,
        in_specs=(
            P(None, "dp", None),
            P(None, "dp", None),
            P("section", None, None, None),
            P("section", None, None, None),
        ),
        out_specs=(P("section", None, "dp", None), P("section", None, "dp", None)),
        check_vma=False,
    )
```

```python
import jax
import jax.numpy as jnp
from jax import lax
from jax.experimental import pallas as pl
from jax.experimental.pallas import tpu as pltpu
from jax.sharding import PartitionSpec as P

norm_epsilon = 1e-06
f32, bf16 = jnp.float32, jnp.bfloat16
MESH = pl.DeviceIdType.MESH
C = 512
M = 4
R = 96
BATCH = 2
OWN = M * R
UNIT = 96 if R % 96 == 0 else (48 if R == 48 else 32)
UNITS = OWN // UNIT
SHARED, PLAIN = (1, 2, 3), (0,)
DMA = pltpu.SemaphoreType.DMA


def dot(a, b):
    return jnp.dot(a, b, preferred_element_type=f32)


def dot_at(a, b):
    return lax.dot_general(a, b, (((0,), (0,)), ((), ())), preferred_element_type=f32)


def kernel(
    img, og, wi, wo, gi_out, go_out,
    WI, WO, WIT, WOT, X, XT, XO, N, H, GP, GY, D, PRE, RS, G, L1, L2, T, LZ,
    loc_w, loc_m, loc_x, ag_s, ag_r, fw_s, fw_r, zf_s, zf_r, g_s, g_r, f_s, f_r, b_s, b_r, n_s, n_r, e_s, e_r, p_s, p_r, q_s, q_r, z_s, z_r,
    near_z, diag,
):
    sec = lax.axis_index("section")
    dp = lax.axis_index("dp")
    y, xl = sec // 2, sec % 2
    xh, z, c = dp // 16, (dp // 2) % 8, dp % 2
    x = xh * 2 + xl

    def dev(x_, y_, z_, c_):
        return (y_ * 2 + x_ % 2, (x_ // 2) * 16 + z_ * 2 + c_)

    right, left = dev((x + 1) % 4, y, z, c), dev((x + 3) % 4, y, z, c)
    up, down = dev(x, (y + 1) % 4, z, c), dev(x, (y + 3) % 4, z, c)
    up_right = dev((x + 1) % 4, (y + 1) % 4, z, c)
    sib = dev(x, y, z, 1 - c)

    def ring_z(off):
        return dev(x, y, (z + off) % 8, c)

    def rc(src, dst, ss, rs, to):
        return pltpu.make_async_remote_copy(
            src_ref=src, dst_ref=dst, send_sem=ss, recv_sem=rs, device_id=to, device_id_type=MESH
        )

    def signal(sem, to):
        pl.semaphore_signal(sem, inc=1, device_id=to, device_id_type=MESH)

    mine, other = 2 * xl, 2 * (1 - xl)

    def load_w(i):
        src, dst = ((wi, WI), (wo, WO))[i]
        return pltpu.make_async_copy(src.at[0], dst.at[pl.ds(mine, 2)], loc_w.at[i])

    def load_rows(i, src, half, dst, sem):
        per = 96 // UNIT
        rows = src.at[i // per, pl.ds(half * 96 + (i % per) * UNIT, UNIT)]
        return pltpu.make_async_copy(rows, dst.at[i * UNIT // R, pl.ds(i * UNIT % R, UNIT)], sem.at[i])

    def load_img(i):
        return load_rows(i, img, xl, X.at[0], loc_m)

    def load_partner_img(i):
        return load_rows(i, img, 1, XT, loc_x)

    def load_og(i):
        return load_rows(i, og, xl, GY.at[4, 0], loc_m)

    load_w(0).start()
    load_w(1).start()

    @pl.when(y == 0)
    def _():
        for i in range(UNITS):
            load_img(i).start()

        @pl.when(xl == 0)
        def _():
            for i in range(UNITS):
                load_partner_img(i).start()

    @pl.when(y == 3)
    def _():
        for i in range(UNITS):
            load_og(i).start()

    bar = pltpu.get_barrier_semaphore()
    peers = [right, left, up, down, sib, ring_z(1), ring_z(7)]
    for to in peers:
        signal(bar, to)
    pl.semaphore_wait(bar, len(peers))

    def z_round(n):
        for off in (1, 7):
            signal(near_z.at[n], ring_z(off))

    z_round(0)

    @pl.when((y == 1) & (xl == 1))
    def _():
        signal(diag, down)

    def ag(t, side):
        src, dst = ((wi, WI), (wo, WO))[t % 2]
        k = t // 2
        if t in SHARED:
            rows = pl.ds(c * 256 + side * 128 + (z % 2) * 64, 64)
        else:
            rows = pl.ds(c * 256 + side * 128, 128)
        return rc(src.at[0, k, rows], dst.at[mine + k, rows], ag_s.at[t, side], ag_r.at[t, side], (right, left)[side])

    def ag_start():
        for t in SHARED + PLAIN:
            for side in range(2):
                ag(t, side).start()

    def zf(t, side):
        here = (WI, WO)[t % 2].at[other + t // 2, pl.ds(c * 256 + side * 128 + (z % 2) * 64, 64)]
        return rc(here, here, zf_s.at[t, side], zf_r.at[t, side], ring_z((1, 7)[side]))

    def fw(t):
        dst = (WI, WO)[t % 2]
        here = dst.at[other + t // 2, pl.ds(c * 256, 256)]
        return rc(here, here, fw_s.at[t], fw_r.at[t], sib)

    def ag_forward():
        for t in SHARED:
            for side in range(2):
                ag(t, side).wait_recv()
                zf(t, side).start()
        for t in PLAIN:
            for side in range(2):
                ag(t, side).wait_recv()
            fw(t).start()
        for t in SHARED:
            for side in range(2):
                zf(t, side).wait_recv()
            fw(t).start()

    def fw_wait():
        for t in range(4):
            fw(t).wait_recv()

    def transpose_weights():
        def one(j, carry):
            WIT[j] = WI[j].T
            WOT[j] = WO[j].T
            return carry

        lax.fori_loop(0, 4, one, 0)

    def put(ref, j, ms, value):
        if isinstance(ms, pl.Slice):
            value = value.reshape(ms.size, R, value.shape[-1])
        ref[j, ms] = value

    def put_own(ref, j, ms, value):
        if isinstance(ms, pl.Slice):
            value = value.reshape(ms.size, R, value.shape[-1])
        ref[j, 0, ms] = value

    def flat(value):
        return value.reshape(-1, value.shape[-1])

    def cell(xb, j, ms, save=True, finish=True):
        wide = xb.astype(f32)
        r = lax.rsqrt(jnp.mean(wide * wide, axis=-1, keepdims=True) + norm_epsilon)
        p = dot(xb, WI[j]) * r
        s = 1.0 / (1.0 + jnp.exp(-p))
        h = p * s
        hb = h.astype(bf16)
        if save:
            put(RS, j, ms, jnp.broadcast_to(r, (r.shape[0], 128)))
            put_own(N, j, ms, (wide * r).astype(bf16))
            put(PRE, j, ms, p)
            put(D, j, ms, s + h * (1.0 - s))
            put_own(H, j, ms, hb)
        if finish:
            return (wide + dot(hb, WO[j])).astype(bf16)

    def f_send(m):
        return rc(X.at[4, m], X.at[0, m], f_s.at[m], f_r.at[m], up)

    def to_left(m):
        return rc(X.at[2, m], XT.at[m], g_s.at[m, 0], g_r.at[m, 1], left)

    def to_right(m):
        return rc(XO.at[m], X.at[2, m], g_s.at[m, 1], g_r.at[m, 0], right)

    def to_up(m):
        return rc(X.at[4, m], X.at[0, m], g_s.at[m, 0], f_r.at[m], up)

    def to_up_right(m):
        return rc(XO.at[m], X.at[0, m], g_s.at[m, 1], f_r.at[m], up_right)

    def first_row(m, carry):
        @pl.when(xl == 1)
        def _():
            to_right(m).wait_recv()

        xb = X[mine, m]
        for i in range(2):
            xb = cell(xb, mine + i, m)
            X[mine + i + 1, m] = xb

        @pl.when(xl == 0)
        def _():
            to_left(m).start()

        @pl.when(xl == 1)
        def _():
            to_up(m).start()
            to_left(m).wait_recv()

        xb = XT[m]
        for i in range(2):
            xb = cell(xb, mine + i, m, save=False)
        XO[m] = xb

        @pl.when(xl == 0)
        def _():
            to_right(m).start()

        @pl.when(xl == 1)
        def _():
            to_up_right(m).start()

        return carry

    def again(m, carry):
        X[other + 1, m] = cell(X[other, m], other, m)
        cell(X[other + 1, m], other + 1, m, finish=False)
        return carry

    def forward(m, carry):
        f_send(m).wait_recv()
        for j in range(4):
            for i in range(2):
                @pl.when((m == 0) & (y == 1) & (xl != j // 2))
                def _():
                    fw(2 * (j % 2) + i).wait_recv()

            X[j + 1, m] = cell(X[j, m], j, m)

        f_send(m).start()
        return carry

    def b_send(m):
        return rc(GY.at[0, 0, m], GY.at[4, 0, m], b_s.at[m], b_r.at[m], down)

    def nh_send(i, io):
        ref, j = (N, H)[io], 2 * i + 1 - c
        return rc(ref.at[j, 0], ref.at[j, 1], n_s.at[i, io], n_r.at[i, io], sib)

    def e_send(i, io, m):
        ref, j = (GP, GY)[io], 2 * i + 1 - c + io
        return rc(ref.at[j, 0, m], ref.at[j, 1, m], e_s.at[i, io, m], e_r.at[i, io, m], sib)

    def cells_back(ms, mlist):
        for j in range(3, -1, -1):
            gy = flat(GY[j + 1, 0, ms])
            gp = (dot(gy, WOT[j]) * flat(D[j, ms])).astype(bf16)
            put_own(GP, j, ms, gp)
            q = jnp.sum(gp.astype(f32) * flat(PRE[j, ms]), axis=-1, keepdims=True) * (1.0 / C)
            gn = dot(gp, WIT[j])
            r = flat(RS[j, ms])[:, :1]
            n = flat(N[j, 0, ms]).astype(f32)
            put_own(GY, j, ms, (gy.astype(f32) + r * (gn - n * q)).astype(bf16))

            @pl.when(c != j % 2)
            def _():
                for m in mlist:
                    e_send(j // 2, 0, m).start()
                    e_send(j // 2, 1, m).start()

    def backward(m, carry):
        b_send(m).wait_recv()
        cells_back(m, [m])

        @pl.when(y > 0)
        def _():
            b_send(m).start()

        return carry

    def last_row(g, carry):
        mlist = [g * BATCH + i for i in range(BATCH)]
        ms = pl.ds(g * BATCH, BATCH)
        for m in mlist:
            f_send(m).wait_recv()
        xb = flat(X[0, ms])
        for j in range(4):
            xb = cell(xb, j, ms, finish=j < 3)
        cells_back(ms, mlist)
        for m in mlist:
            b_send(m).start()
        return carry

    @pl.when((y > 0) | (xl == 1))
    def _():
        ag_start()

    load_w(0).wait()
    load_w(1).wait()

    @pl.when(y == 0)
    def _():
        @pl.when(xl == 1)
        def _():
            pl.semaphore_wait(diag, 1)

        @pl.when(xl == 0)
        def _():
            for i in range(UNITS):
                load_img(i).wait()
                load_partner_img(i).wait()

        lax.fori_loop(0, M, first_row, 0)

        @pl.when(xl == 0)
        def _():
            ag_start()

        ag_forward()
        fw_wait()

        @pl.when(xl == 1)
        def _():
            for i in range(UNITS):
                load_img(i).wait()

        lax.fori_loop(0, M, again, 0)

    @pl.when(y > 0)
    def _():
        ag_forward()

        @pl.when(y > 1)
        def _():
            fw_wait()
            transpose_weights()

        @pl.when(y < 3)
        def _():
            lax.fori_loop(0, M, forward, 0)

        @pl.when(y == 3)
        def _():
            for i in range(UNITS):
                load_og(i).wait()
            lax.fori_loop(0, M // BATCH, last_row, 0)

    @pl.when(y < 2)
    def _():
        transpose_weights()

    for i in range(2):
        for io in range(2):
            nh_send(i, io).start()
    pl.semaphore_wait(near_z.at[0], 2)
    z_round(1)

    @pl.when(y < 3)
    def _():
        lax.fori_loop(0, 1, backward, 0)

    pl.semaphore_wait(near_z.at[1], 2)
    z_round(2)

    @pl.when(y < 3)
    def _():
        lax.fori_loop(1, 2, backward, 0)

    pl.semaphore_wait(near_z.at[2], 2)
    z_round(3)

    @pl.when(y < 3)
    def _():
        lax.fori_loop(2, M, backward, 0)

    def weight(i, io):
        j = 2 * i + c
        for arr in (0, 1) if io == 0 else ():
            nh_send(i, arr).wait_recv()
            for m in range(M):
                e_send(i, arr, m).wait_recv()
        a, b = ((N.at[j], GP.at[j]), (H.at[j], GY.at[j + 1]))[io]
        g = dot_at(a[...].reshape(2 * OWN, C), b[...].reshape(2 * OWN, C))
        G[i, io] = g.astype(bf16).reshape(2, 8, 2, 16, C)

    xh_r, xh_l = ((x + 1) % 4) // 2, ((x + 3) % 4) // 2
    core = (c, 1 - c)

    def l1(io, e, side):
        return rc(
            G.at[xl, io, 1 - xh, pl.ds(side * 4, 4), core[e]], L1.at[io, e, side],
            p_s.at[io, e, side], p_r.at[io, e, side], (right, left)[side],
        )

    def l2(io, e, side, half):
        rows = pl.ds(half * 4, 4)
        return rc(
            G.at[1 - xl, io, (xh_r, xh_l)[side], rows, core[e]], L2.at[io, e, side, rows],
            q_s.at[io, e, side, half], q_r.at[io, e, side, half], (right, left)[side],
        )

    def first_sends(i, io):
        @pl.when(xl == i)
        def _():
            for e in range(2):
                l1(io, e, 0).start()
                l1(io, e, 1).start()

        @pl.when(xl != i)
        def _():
            for e in range(2):
                l2(io, e, 0, 1).start()
                l2(io, e, 1, 0).start()

    def relay(io, e):
        for side, xd in ((0, xh_r), (1, xh_l)):
            l1(io, e, side).wait_recv()
            rows = pl.ds(side * 4, 4)
            G[1 - xl, io, xd, rows, core[e]] = (
                G[1 - xl, io, xd, rows, core[e]].astype(f32) + L1[io, e, side].astype(f32)
            ).astype(bf16)
            l2(io, e, side, side).start()

    def z_send(io, e, off):
        return rc(
            T.at[io, e, (z + off) % 8], LZ.at[io, e, off],
            z_s.at[io, e, off], z_r.at[io, e, off], dev(x, y, (z + off) % 8, core[e]),
        )

    offs = ((4, 3, 5, 2, 6, 1, 7), (4, 3, 5, 2, 6, 1, 7, 0))

    def collect(io, e):
        for side in range(2):
            for half in range(2):
                l2(io, e, side, half).wait_recv()
        T[io, e] = (
            G[xl, io, xh, :, core[e]].astype(f32) + L2[io, e, 0].astype(f32) + L2[io, e, 1].astype(f32)
        ).astype(bf16)
        for off in offs[e]:
            z_send(io, e, off).start()

    weight(1, 0)
    first_sends(1, 0)
    weight(0, 0)
    first_sends(0, 0)
    weight(1, 1)
    weight(0, 1)
    relay(0, 0)
    relay(0, 1)
    first_sends(1, 1)
    first_sends(0, 1)
    pl.semaphore_wait(near_z.at[3], 2)
    collect(0, 0)
    collect(0, 1)
    relay(1, 0)
    relay(1, 1)
    collect(1, 0)
    collect(1, 1)

    for io in range(2):
        for e in range(2):
            total = T[io, 0, z].astype(f32) if e == 0 else 0.0
            for off in offs[e]:
                z_send(io, e, off).wait_recv()
                total = total + LZ[io, e, off].astype(f32)
            (gi_out, go_out)[io][core[e]] = total

    for t in range(4):
        for side in range(2):
            ag(t, side).wait_send()
        fw(t).wait_send()
    for t in SHARED:
        for side in range(2):
            zf(t, side).wait_send()

    @pl.when(y == 0)
    def _():
        for m in range(M):
            to_left(m).wait_send()
            to_right(m).wait_send()

    @pl.when((y > 0) & (y < 3))
    def _():
        for m in range(M):
            f_send(m).wait_send()

    @pl.when(y > 0)
    def _():
        for m in range(M):
            b_send(m).wait_send()

    for io in range(2):
        for i in range(2):
            nh_send(i, io).wait_send()
            for m in range(M):
                e_send(i, io, m).wait_send()
        for e in range(2):
            for side in range(2):
                l1(io, e, side).wait_send()
                for half in range(2):
                    l2(io, e, side, half).wait_send()
            for off in offs[e]:
                z_send(io, e, off).wait_send()


def local(images, out_grad, w_in, w_out):
    V = pltpu.VMEM
    REG = pltpu.SemaphoreType.REGULAR
    weights = V((4, C, C), bf16)
    acts = V((4, 2, M, R, C), bf16)
    wide = V((4, M, R, C), f32)
    scratch = [
        weights, weights, weights, weights,
        V((5, M, R, C), bf16), V((M, R, C), bf16), V((M, R, C), bf16),
        acts, acts, acts, V((5, 2, M, R, C), bf16), wide, wide, V((4, M, R, 128), f32),
        V((2, 2, 2, 8, 2, 16, C), bf16),
        V((2, 2, 2, 4, 16, C), bf16), V((2, 2, 2, 8, 16, C), bf16), V((2, 2, 8, 16, C), bf16),
        V((2, 2, 8, 16, C), bf16),
        DMA((2,)), DMA((UNITS,)), DMA((UNITS,)), DMA((4, 2)), DMA((4, 2)), DMA((4,)), DMA((4,)), DMA((4, 2)), DMA((4, 2)),
        DMA((M, 2)), DMA((M, 2)), DMA((M,)), DMA((M,)), DMA((M,)), DMA((M,)),
        DMA((2, 2)), DMA((2, 2)), DMA((2, 2, M)), DMA((2, 2, M)),
        DMA((2, 2, 2)), DMA((2, 2, 2)), DMA((2, 2, 2, 2)), DMA((2, 2, 2, 2)), DMA((2, 2, 8)), DMA((2, 2, 8)),
        REG((4,)), REG,
    ]
    out = jax.ShapeDtypeStruct((2, 16, C), f32)
    grad_in, grad_out = pl.pallas_call(
        kernel,
        out_shape=(out, out),
        in_specs=[pl.BlockSpec(memory_space=pltpu.HBM)] * 4,
        out_specs=(pl.BlockSpec(memory_space=pltpu.VMEM),) * 2,
        scratch_shapes=scratch,
        compiler_params=pltpu.CompilerParams(
            collective_id=0, has_side_effects=True, vmem_limit_bytes=60 * 2**20
        ),
        name="window",
    )(images, out_grad, w_in, w_out)
    return grad_in[None], grad_out[None]


def solution(mesh):
    return jax.shard_map(
        local,
        mesh=mesh,
        in_specs=(
            P(None, "dp", None),
            P(None, "dp", None),
            P("section", None, None, None),
            P("section", None, None, None),
        ),
        out_specs=(P("section", None, "dp", None), P("section", None, "dp", None)),
        check_vma=False,
    )
```

```python
import jax
import jax.numpy as jnp
from jax import lax
from jax.experimental import pallas as pl
from jax.experimental.pallas import tpu as pltpu
from jax.sharding import PartitionSpec as P

norm_epsilon = 1e-06
f32, bf16 = jnp.float32, jnp.bfloat16
MESH = pl.DeviceIdType.MESH
C = 512
M = 4
R = 96
BATCH = 2
OWN = M * R
UNIT = 96 if R % 96 == 0 else (48 if R == 48 else 32)
UNITS = OWN // UNIT
SHARED, PLAIN = (1, 2, 3), (0,)
DMA = pltpu.SemaphoreType.DMA


def dot(a, b):
    return jnp.dot(a, b, preferred_element_type=f32)


def dot_at(a, b):
    return lax.dot_general(a, b, (((0,), (0,)), ((), ())), preferred_element_type=f32)


def kernel(
    img, og, wi, wo, gi_out, go_out,
    WI, WO, WIT, WOT, X, XT, XO, N, H, GP, GY, D, PRE, RS, G, L1, L2, T, LZ, ZP, ZM, Q, LX,
    loc_w, loc_m, loc_x, ag_s, ag_r, fw_s, fw_r, zf_s, zf_r, g_s, g_r, f_s, f_r, b_s, b_r, n_s, n_r, e_s, e_r, p_s, p_r, q_s, q_r, z_s, z_r,
    zp_s, zp_r, zm_s, zm_r, lx_s, lx_r, near_z, diag,
):
    sec = lax.axis_index("section")
    dp = lax.axis_index("dp")
    y, xl = sec // 2, sec % 2
    xh, z, c = dp // 16, (dp // 2) % 8, dp % 2
    x = xh * 2 + xl

    def dev(x_, y_, z_, c_):
        return (y_ * 2 + x_ % 2, (x_ // 2) * 16 + z_ * 2 + c_)

    right, left = dev((x + 1) % 4, y, z, c), dev((x + 3) % 4, y, z, c)
    up, down = dev(x, (y + 1) % 4, z, c), dev(x, (y + 3) % 4, z, c)
    up_right = dev((x + 1) % 4, (y + 1) % 4, z, c)
    sib = dev(x, y, z, 1 - c)

    def ring_z(off):
        return dev(x, y, (z + off) % 8, c)

    def rc(src, dst, ss, rs, to):
        return pltpu.make_async_remote_copy(
            src_ref=src, dst_ref=dst, send_sem=ss, recv_sem=rs, device_id=to, device_id_type=MESH
        )

    def signal(sem, to):
        pl.semaphore_signal(sem, inc=1, device_id=to, device_id_type=MESH)

    mine, other = 2 * xl, 2 * (1 - xl)

    def load_w(i):
        src, dst = ((wi, WI), (wo, WO))[i]
        return pltpu.make_async_copy(src.at[0], dst.at[pl.ds(mine, 2)], loc_w.at[i])

    def load_rows(i, src, half, dst, sem):
        per = 96 // UNIT
        rows = src.at[i // per, pl.ds(half * 96 + (i % per) * UNIT, UNIT)]
        return pltpu.make_async_copy(rows, dst.at[i * UNIT // R, pl.ds(i * UNIT % R, UNIT)], sem.at[i])

    def load_img(i):
        return load_rows(i, img, xl, X.at[0], loc_m)

    def load_partner_img(i):
        return load_rows(i, img, 1, XT, loc_x)

    def load_og(i):
        return load_rows(i, og, xl, GY.at[4, 0], loc_m)

    load_w(0).start()
    load_w(1).start()

    @pl.when(y == 0)
    def _():
        for i in range(UNITS):
            load_img(i).start()

        @pl.when(xl == 0)
        def _():
            for i in range(UNITS):
                load_partner_img(i).start()

    @pl.when(y == 3)
    def _():
        for i in range(UNITS):
            load_og(i).start()

    bar = pltpu.get_barrier_semaphore()
    peers = [right, left, up, down, sib, ring_z(1), ring_z(7)]
    for to in peers:
        signal(bar, to)
    pl.semaphore_wait(bar, len(peers))

    def z_round(n):
        for off in (1, 7):
            signal(near_z.at[n], ring_z(off))

    z_round(0)

    @pl.when((y == 1) & (xl == 1))
    def _():
        signal(diag, down)

    def ag(t, side):
        src, dst = ((wi, WI), (wo, WO))[t % 2]
        k = t // 2
        if t in SHARED:
            rows = pl.ds(c * 256 + side * 128 + (z % 2) * 64, 64)
        else:
            rows = pl.ds(c * 256 + side * 128, 128)
        return rc(src.at[0, k, rows], dst.at[mine + k, rows], ag_s.at[t, side], ag_r.at[t, side], (right, left)[side])

    def ag_start():
        for t in SHARED + PLAIN:
            for side in range(2):
                ag(t, side).start()

    def zf(t, side):
        here = (WI, WO)[t % 2].at[other + t // 2, pl.ds(c * 256 + side * 128 + (z % 2) * 64, 64)]
        return rc(here, here, zf_s.at[t, side], zf_r.at[t, side], ring_z((1, 7)[side]))

    def fw(t):
        dst = (WI, WO)[t % 2]
        here = dst.at[other + t // 2, pl.ds(c * 256, 256)]
        return rc(here, here, fw_s.at[t], fw_r.at[t], sib)

    def ag_forward():
        for t in SHARED:
            for side in range(2):
                ag(t, side).wait_recv()
                zf(t, side).start()
        for t in PLAIN:
            for side in range(2):
                ag(t, side).wait_recv()
            fw(t).start()
        for t in SHARED:
            for side in range(2):
                zf(t, side).wait_recv()
            fw(t).start()

    def fw_wait():
        for t in range(4):
            fw(t).wait_recv()

    def transpose_weights():
        def one(j, carry):
            WIT[j] = WI[j].T
            WOT[j] = WO[j].T
            return carry

        lax.fori_loop(0, 4, one, 0)

    def put(ref, j, ms, value):
        if isinstance(ms, pl.Slice):
            value = value.reshape(ms.size, R, value.shape[-1])
        ref[j, ms] = value

    def put_own(ref, j, ms, value):
        if isinstance(ms, pl.Slice):
            value = value.reshape(ms.size, R, value.shape[-1])
        ref[j, 0, ms] = value

    def flat(value):
        return value.reshape(-1, value.shape[-1])

    def cell(xb, j, ms, save=True, finish=True):
        wide = xb.astype(f32)
        r = lax.rsqrt(jnp.mean(wide * wide, axis=-1, keepdims=True) + norm_epsilon)
        p = dot(xb, WI[j]) * r
        s = 0.5 * jnp.tanh(0.5 * p) + 0.5
        h = p * s
        hb = h.astype(bf16)
        if save:
            put(RS, j, ms, jnp.broadcast_to(r, (r.shape[0], 128)))
            put_own(N, j, ms, (wide * r).astype(bf16))
            put(PRE, j, ms, p)
            put(D, j, ms, s + h * (1.0 - s))
            put_own(H, j, ms, hb)
        if finish:
            return (wide + dot(hb, WO[j])).astype(bf16)

    def f_send(m):
        return rc(X.at[4, m], X.at[0, m], f_s.at[m], f_r.at[m], up)

    def to_left(m):
        return rc(X.at[2, m], XT.at[m], g_s.at[m, 0], g_r.at[m, 1], left)

    def to_right(m):
        return rc(XO.at[m], X.at[2, m], g_s.at[m, 1], g_r.at[m, 0], right)

    def to_up(m):
        return rc(X.at[4, m], X.at[0, m], g_s.at[m, 0], f_r.at[m], up)

    def to_up_right(m):
        return rc(XO.at[m], X.at[0, m], g_s.at[m, 1], f_r.at[m], up_right)

    def first_row(m, carry):
        @pl.when(xl == 1)
        def _():
            to_right(m).wait_recv()

        xb = X[mine, m]
        for i in range(2):
            xb = cell(xb, mine + i, m)
            X[mine + i + 1, m] = xb

        @pl.when(xl == 0)
        def _():
            to_left(m).start()

        @pl.when(xl == 1)
        def _():
            to_up(m).start()
            to_left(m).wait_recv()

        xb = XT[m]
        for i in range(2):
            xb = cell(xb, mine + i, m, save=False)
        XO[m] = xb

        @pl.when(xl == 0)
        def _():
            to_right(m).start()

        @pl.when(xl == 1)
        def _():
            to_up_right(m).start()

        return carry

    def again(m, carry):
        X[other + 1, m] = cell(X[other, m], other, m)
        cell(X[other + 1, m], other + 1, m, finish=False)
        return carry

    def forward(m, carry):
        f_send(m).wait_recv()
        for j in range(4):
            for i in range(2):
                @pl.when((m == 0) & (y == 1) & (xl != j // 2))
                def _():
                    fw(2 * (j % 2) + i).wait_recv()

            X[j + 1, m] = cell(X[j, m], j, m)

        f_send(m).start()
        return carry

    def b_send(m):
        return rc(GY.at[0, 0, m], GY.at[4, 0, m], b_s.at[m], b_r.at[m], down)

    def nh_send(i, io):
        ref, j = (N, H)[io], 2 * i + 1 - c
        return rc(ref.at[j, 0], ref.at[j, 1], n_s.at[i, io], n_r.at[i, io], sib)

    def e_send(i, io, m):
        ref, j = (GP, GY)[io], 2 * i + 1 - c + io
        return rc(ref.at[j, 0, m], ref.at[j, 1, m], e_s.at[i, io, m], e_r.at[i, io, m], sib)

    def cells_back(ms, mlist):
        for j in range(3, -1, -1):
            gy = flat(GY[j + 1, 0, ms])
            gp = (dot(gy, WOT[j]) * flat(D[j, ms])).astype(bf16)
            put_own(GP, j, ms, gp)
            q = jnp.sum(gp.astype(f32) * flat(PRE[j, ms]), axis=-1, keepdims=True) * (1.0 / C)
            gn = dot(gp, WIT[j])
            r = flat(RS[j, ms])[:, :1]
            n = flat(N[j, 0, ms]).astype(f32)
            put_own(GY, j, ms, (gy.astype(f32) + r * (gn - n * q)).astype(bf16))

            @pl.when(c != j % 2)
            def _():
                for m in mlist:
                    e_send(j // 2, 0, m).start()
                    e_send(j // 2, 1, m).start()

    def backward(m, carry):
        b_send(m).wait_recv()
        cells_back(m, [m])

        @pl.when(y > 0)
        def _():
            b_send(m).start()

        return carry

    def last_row(g, carry):
        mlist = [g * BATCH + i for i in range(BATCH)]
        ms = pl.ds(g * BATCH, BATCH)
        for m in mlist:
            f_send(m).wait_recv()
        xb = flat(X[0, ms])
        for j in range(4):
            xb = cell(xb, j, ms, finish=j < 3)
        cells_back(ms, mlist)
        for m in mlist:
            b_send(m).start()
        return carry

    @pl.when((y > 0) | (xl == 1))
    def _():
        ag_start()

    load_w(0).wait()
    load_w(1).wait()

    @pl.when(y == 0)
    def _():
        @pl.when(xl == 1)
        def _():
            pl.semaphore_wait(diag, 1)

        @pl.when(xl == 0)
        def _():
            for i in range(UNITS):
                load_img(i).wait()
                load_partner_img(i).wait()

        lax.fori_loop(0, M, first_row, 0)

        @pl.when(xl == 0)
        def _():
            ag_start()

        ag_forward()
        fw_wait()

        @pl.when(xl == 1)
        def _():
            for i in range(UNITS):
                load_img(i).wait()

        lax.fori_loop(0, M, again, 0)

    @pl.when(y > 0)
    def _():
        ag_forward()

        @pl.when(y > 1)
        def _():
            fw_wait()
            transpose_weights()

        @pl.when(y < 3)
        def _():
            lax.fori_loop(0, M, forward, 0)

        @pl.when(y == 3)
        def _():
            for i in range(UNITS):
                load_og(i).wait()
            lax.fori_loop(0, M // BATCH, last_row, 0)

    @pl.when(y < 2)
    def _():
        transpose_weights()

    for i in range(2):
        for io in range(2):
            nh_send(i, io).start()
    pl.semaphore_wait(near_z.at[0], 2)
    z_round(1)

    @pl.when(y < 3)
    def _():
        lax.fori_loop(0, 1, backward, 0)

    pl.semaphore_wait(near_z.at[1], 2)
    z_round(2)

    @pl.when(y < 3)
    def _():
        lax.fori_loop(1, 2, backward, 0)

    pl.semaphore_wait(near_z.at[2], 2)
    z_round(3)

    @pl.when(y < 3)
    def _():
        lax.fori_loop(2, M, backward, 0)

    def weight(i, io):
        j = 2 * i + c
        for arr in (0, 1) if io == 1 else ():
            nh_send(i, arr).wait_recv()
            for m in range(M):
                e_send(i, arr, m).wait_recv()
        a, b = ((N.at[j], GP.at[j]), (H.at[j], GY.at[j + 1]))[io]
        g = dot_at(a[...].reshape(2 * OWN, C), b[...].reshape(2 * OWN, C))
        G[i, io] = g.astype(bf16).reshape(2, 8, 2, 16, C)

    xh_r, xh_l = ((x + 1) % 4) // 2, ((x + 3) % 4) // 2
    core = (c, 1 - c)

    def l1(io, e, side):
        return rc(
            G.at[xl, io, 1 - xh, pl.ds(side * 4, 4), core[e]], L1.at[io, e, side],
            p_s.at[io, e, side], p_r.at[io, e, side], (right, left)[side],
        )

    def l2(io, e, side, half):
        rows = pl.ds(half * 4, 4)
        return rc(
            G.at[1 - xl, io, (xh_r, xh_l)[side], rows, core[e]], L2.at[io, e, side, rows],
            q_s.at[io, e, side, half], q_r.at[io, e, side, half], (right, left)[side],
        )

    def first_sends(i, io, e):
        @pl.when(xl == i)
        def _():
            l1(io, e, 0).start()
            l1(io, e, 1).start()

        @pl.when(xl != i)
        def _():
            l2(io, e, 0, 1).start()
            l2(io, e, 1, 0).start()

    def relay(io, e):
        for side, xd in ((0, xh_r), (1, xh_l)):
            l1(io, e, side).wait_recv()
            rows = pl.ds(side * 4, 4)
            G[1 - xl, io, xd, rows, core[e]] = (
                G[1 - xl, io, xd, rows, core[e]].astype(f32) + L1[io, e, side].astype(f32)
            ).astype(bf16)
            l2(io, e, side, side).start()

    def z_send(io, e, off):
        return rc(
            T.at[io, e, (z + off) % 8], LZ.at[io, e, off],
            z_s.at[io, e, off], z_r.at[io, e, off], dev(x, y, (z + off) % 8, core[e]),
        )

    offs = ((4, 3, 5, 2, 6, 1, 7), (4, 3, 5, 2, 6, 1, 7, 0))

    def collect(io, e):
        for side in range(2):
            for half in range(2):
                l2(io, e, side, half).wait_recv()
        T[io, e] = (
            G[xl, io, xh, :, core[e]].astype(f32) + L2[io, e, 0].astype(f32) + L2[io, e, 1].astype(f32)
        ).astype(bf16)
        for off in offs[e]:
            z_send(io, e, off).start()

    def part(chunk):
        return (slice(None), 1, slice(None), chunk, c)

    def zp(n):
        return rc(G.at[part((z + 4 - n) % 8)], ZP.at[n], zp_s.at[n], zp_r.at[n], ring_z(1))

    def zm(n):
        return rc(G.at[part((z + 5 + n) % 8)], ZM.at[n], zm_s.at[n], zm_r.at[n], ring_z(7))

    def ring_step(n):
        zp(n).wait_recv()
        here = part((z + 3 - n) % 8)
        G[here] = (G[here].astype(f32) + ZP[n].astype(f32)).astype(bf16)
        zp(n + 1).start()
        if n < 2:
            zm(n).wait_recv()
            here = part((z + 6 + n) % 8)
            G[here] = (G[here].astype(f32) + ZM[n].astype(f32)).astype(bf16)
            zm(n + 1).start()

    def lx(off):
        to = (x + off) % 4
        return rc(Q.at[to % 2, to // 2], LX.at[off - 1], lx_s.at[off - 1], lx_r.at[off - 1], dev(to, y, z, c))

    weight(1, 1)
    first_sends(1, 1, 1)
    weight(0, 1)
    zp(0).start()
    zm(0).start()
    first_sends(0, 1, 1)
    weight(1, 0)
    first_sends(1, 0, 0)
    weight(0, 0)
    first_sends(0, 0, 0)
    relay(1, 1)
    first_sends(1, 0, 1)
    first_sends(0, 0, 1)
    ring_step(0)
    pl.semaphore_wait(near_z.at[3], 2)
    relay(0, 0)
    collect(1, 1)
    ring_step(1)
    relay(0, 1)
    collect(0, 0)
    ring_step(2)
    collect(0, 1)
    zp(3).wait_recv()
    zm(2).wait_recv()
    Q[...] = (G[part(z)].astype(f32) + ZP[3].astype(f32) + ZM[2].astype(f32)).astype(bf16)
    for off in (2, 1, 3):
        lx(off).start()

    for io, e in ((1, 1), (0, 0), (0, 1)):
        total = T[io, 0, z].astype(f32) if e == 0 else 0.0
        for off in offs[e]:
            z_send(io, e, off).wait_recv()
            total = total + LZ[io, e, off].astype(f32)
        (gi_out, go_out)[io][core[e]] = total
    total = Q[xl, xh].astype(f32)
    for off in range(1, 4):
        lx(off).wait_recv()
        total = total + LX[off - 1].astype(f32)
    go_out[c] = total

    for t in range(4):
        for side in range(2):
            ag(t, side).wait_send()
        fw(t).wait_send()
    for t in SHARED:
        for side in range(2):
            zf(t, side).wait_send()

    @pl.when(y == 0)
    def _():
        for m in range(M):
            to_left(m).wait_send()
            to_right(m).wait_send()

    @pl.when((y > 0) & (y < 3))
    def _():
        for m in range(M):
            f_send(m).wait_send()

    @pl.when(y > 0)
    def _():
        for m in range(M):
            b_send(m).wait_send()

    for io in range(2):
        for i in range(2):
            nh_send(i, io).wait_send()
            for m in range(M):
                e_send(i, io, m).wait_send()
    for io, e in ((1, 1), (0, 0), (0, 1)):
        for side in range(2):
            l1(io, e, side).wait_send()
            for half in range(2):
                l2(io, e, side, half).wait_send()
        for off in offs[e]:
            z_send(io, e, off).wait_send()
    for n in range(4):
        zp(n).wait_send()
    for n in range(3):
        zm(n).wait_send()
        lx(n + 1).wait_send()


def local(images, out_grad, w_in, w_out):
    V = pltpu.VMEM
    REG = pltpu.SemaphoreType.REGULAR
    weights = V((4, C, C), bf16)
    acts = V((4, 2, M, R, C), bf16)
    wide = V((4, M, R, C), f32)
    scratch = [
        weights, weights, weights, weights,
        V((5, M, R, C), bf16), V((M, R, C), bf16), V((M, R, C), bf16),
        acts, acts, acts, V((5, 2, M, R, C), bf16), wide, wide, V((4, M, R, 128), f32),
        V((2, 2, 2, 8, 2, 16, C), bf16),
        V((2, 2, 2, 4, 16, C), bf16), V((2, 2, 2, 8, 16, C), bf16), V((2, 2, 8, 16, C), bf16),
        V((2, 2, 8, 16, C), bf16),
        V((4, 2, 2, 16, C), bf16), V((3, 2, 2, 16, C), bf16), V((2, 2, 16, C), bf16), V((3, 16, C), bf16),
        DMA((2,)), DMA((UNITS,)), DMA((UNITS,)), DMA((4, 2)), DMA((4, 2)), DMA((4,)), DMA((4,)), DMA((4, 2)), DMA((4, 2)),
        DMA((M, 2)), DMA((M, 2)), DMA((M,)), DMA((M,)), DMA((M,)), DMA((M,)),
        DMA((2, 2)), DMA((2, 2)), DMA((2, 2, M)), DMA((2, 2, M)),
        DMA((2, 2, 2)), DMA((2, 2, 2)), DMA((2, 2, 2, 2)), DMA((2, 2, 2, 2)), DMA((2, 2, 8)), DMA((2, 2, 8)),
        DMA((4,)), DMA((4,)), DMA((3,)), DMA((3,)), DMA((3,)), DMA((3,)),
        REG((4,)), REG,
    ]
    out = jax.ShapeDtypeStruct((2, 16, C), f32)
    grad_in, grad_out = pl.pallas_call(
        kernel,
        out_shape=(out, out),
        in_specs=[pl.BlockSpec(memory_space=pltpu.HBM)] * 4,
        out_specs=(pl.BlockSpec(memory_space=pltpu.VMEM),) * 2,
        scratch_shapes=scratch,
        compiler_params=pltpu.CompilerParams(
            collective_id=0, has_side_effects=True, vmem_limit_bytes=60 * 2**20
        ),
        name="window",
    )(images, out_grad, w_in, w_out)
    return grad_in[None], grad_out[None]


def solution(mesh):
    return jax.shard_map(
        local,
        mesh=mesh,
        in_specs=(
            P(None, "dp", None),
            P(None, "dp", None),
            P("section", None, None, None),
            P("section", None, None, None),
        ),
        out_specs=(P("section", None, "dp", None), P("section", None, "dp", None)),
        check_vma=False,
    )
```

```python
import jax
import jax.numpy as jnp
from jax import lax
from jax.experimental import pallas as pl
from jax.experimental.pallas import tpu as pltpu
from jax.sharding import PartitionSpec as P

norm_epsilon = 1e-06
f32, bf16 = jnp.float32, jnp.bfloat16
MESH = pl.DeviceIdType.MESH
C = 512
M = 4
R = 96
BATCH = 2
OWN = M * R
UNIT = 96 if R % 96 == 0 else (48 if R == 48 else 32)
UNITS = OWN // UNIT
SHARED, PLAIN = (1, 2, 3), (0,)
DMA = pltpu.SemaphoreType.DMA


def dot(a, b):
    return jnp.dot(a, b, preferred_element_type=f32)


def dot_at(a, b):
    return lax.dot_general(a, b, (((0,), (0,)), ((), ())), preferred_element_type=f32)


def kernel(
    img, og, wi, wo, out,
    WI, WO, WIT, WOT, X, XT, XO, N, H, GP, GY, D, PRE, RS, G, L1, L2, T, LZ, ZP, ZM, Q, LX,
    loc_w, loc_m, loc_x, ag_s, ag_r, fw_s, fw_r, zf_s, zf_r, g_s, g_r, f_s, f_r, b_s, b_r, n_s, n_r, e_s, e_r, p_s, p_r, q_s, q_r, z_s, z_r,
    zp_s, zp_r, zm_s, zm_r, lx_s, lx_r, near_z, diag,
):
    sec = lax.axis_index("section")
    dp = lax.axis_index("dp")
    y, xl = sec // 2, sec % 2
    xh, z, c = dp // 16, (dp // 2) % 8, dp % 2
    x = xh * 2 + xl

    def dev(x_, y_, z_, c_):
        return (y_ * 2 + x_ % 2, (x_ // 2) * 16 + z_ * 2 + c_)

    right, left = dev((x + 1) % 4, y, z, c), dev((x + 3) % 4, y, z, c)
    up, down = dev(x, (y + 1) % 4, z, c), dev(x, (y + 3) % 4, z, c)
    up_right = dev((x + 1) % 4, (y + 1) % 4, z, c)
    sib = dev(x, y, z, 1 - c)

    def ring_z(off):
        return dev(x, y, (z + off) % 8, c)

    def rc(src, dst, ss, rs, to):
        return pltpu.make_async_remote_copy(
            src_ref=src, dst_ref=dst, send_sem=ss, recv_sem=rs, device_id=to, device_id_type=MESH
        )

    def signal(sem, to):
        pl.semaphore_signal(sem, inc=1, device_id=to, device_id_type=MESH)

    mine, other = 2 * xl, 2 * (1 - xl)

    def load_w(i):
        src, dst = ((wi, WI), (wo, WO))[i]
        return pltpu.make_async_copy(src.at[0], dst.at[pl.ds(mine, 2)], loc_w.at[i])

    def load_rows(i, src, half, dst, sem):
        per = 96 // UNIT
        rows = src.at[i // per, pl.ds(half * 96 + (i % per) * UNIT, UNIT)]
        return pltpu.make_async_copy(rows, dst.at[i * UNIT // R, pl.ds(i * UNIT % R, UNIT)], sem.at[i])

    def load_img(i):
        return load_rows(i, img, xl, X.at[0], loc_m)

    def load_partner_img(i):
        return load_rows(i, img, 1, XT, loc_x)

    def load_og(i):
        return load_rows(i, og, xl, GY.at[4, 0], loc_m)

    load_w(0).start()
    load_w(1).start()

    @pl.when(y == 0)
    def _():
        for i in range(UNITS):
            load_img(i).start()

        @pl.when(xl == 0)
        def _():
            for i in range(UNITS):
                load_partner_img(i).start()

    @pl.when(y == 3)
    def _():
        for i in range(UNITS):
            load_og(i).start()

    bar = pltpu.get_barrier_semaphore()
    peers = [right, left, up, down, sib, ring_z(1), ring_z(7)]
    for to in peers:
        signal(bar, to)
    pl.semaphore_wait(bar, len(peers))

    def z_round(n):
        for off in (1, 7):
            signal(near_z.at[n], ring_z(off))

    z_round(0)

    @pl.when((y == 1) & (xl == 1))
    def _():
        signal(diag, down)

    def ag(t, side):
        src, dst = ((wi, WI), (wo, WO))[t % 2]
        k = t // 2
        if t in SHARED:
            rows = pl.ds(c * 256 + side * 128 + (z % 2) * 64, 64)
        else:
            rows = pl.ds(c * 256 + side * 128, 128)
        return rc(src.at[0, k, rows], dst.at[mine + k, rows], ag_s.at[t, side], ag_r.at[t, side], (right, left)[side])

    def ag_start():
        for t in SHARED + PLAIN:
            for side in range(2):
                ag(t, side).start()

    def zf(t, side):
        here = (WI, WO)[t % 2].at[other + t // 2, pl.ds(c * 256 + side * 128 + (z % 2) * 64, 64)]
        return rc(here, here, zf_s.at[t, side], zf_r.at[t, side], ring_z((1, 7)[side]))

    def fw(t):
        dst = (WI, WO)[t % 2]
        here = dst.at[other + t // 2, pl.ds(c * 256, 256)]
        return rc(here, here, fw_s.at[t], fw_r.at[t], sib)

    def ag_forward():
        for t in SHARED:
            for side in range(2):
                ag(t, side).wait_recv()
                zf(t, side).start()
        for t in PLAIN:
            for side in range(2):
                ag(t, side).wait_recv()
            fw(t).start()
        for t in SHARED:
            for side in range(2):
                zf(t, side).wait_recv()
            fw(t).start()

    def fw_wait():
        for t in range(4):
            fw(t).wait_recv()

    def transpose_weights():
        def one(j, carry):
            WIT[j] = WI[j].T
            WOT[j] = WO[j].T
            return carry

        lax.fori_loop(0, 4, one, 0)

    def put(ref, j, ms, value):
        if isinstance(ms, pl.Slice):
            value = value.reshape(ms.size, R, value.shape[-1])
        ref[j, ms] = value

    def put_own(ref, j, ms, value):
        if isinstance(ms, pl.Slice):
            value = value.reshape(ms.size, R, value.shape[-1])
        ref[j, 0, ms] = value

    def flat(value):
        return value.reshape(-1, value.shape[-1])

    def cell(xb, j, ms, save=True, finish=True):
        wide = xb.astype(f32)
        r = lax.rsqrt(jnp.mean(wide * wide, axis=-1, keepdims=True) + norm_epsilon)
        p = dot(xb, WI[j]) * r
        s = 0.5 * jnp.tanh(0.5 * p) + 0.5
        h = p * s
        hb = h.astype(bf16)
        if save:
            put(RS, j, ms, jnp.broadcast_to(r, (r.shape[0], 128)))
            put_own(N, j, ms, (wide * r).astype(bf16))
            put(PRE, j, ms, p)
            put(D, j, ms, s + h * (1.0 - s))
            put_own(H, j, ms, hb)
        if finish:
            return (wide + dot(hb, WO[j])).astype(bf16)

    def f_send(m):
        return rc(X.at[4, m], X.at[0, m], f_s.at[m], f_r.at[m], up)

    def to_left(m):
        return rc(X.at[2, m], XT.at[m], g_s.at[m, 0], g_r.at[m, 1], left)

    def to_right(m):
        return rc(XO.at[m], X.at[2, m], g_s.at[m, 1], g_r.at[m, 0], right)

    def to_up(m):
        return rc(X.at[4, m], X.at[0, m], g_s.at[m, 0], f_r.at[m], up)

    def to_up_right(m):
        return rc(XO.at[m], X.at[0, m], g_s.at[m, 1], f_r.at[m], up_right)

    def own_stream(m):
        xb = X[mine, m]
        for i in range(2):
            xb = cell(xb, mine + i, m)
            X[mine + i + 1, m] = xb

    def partner_stream(m):
        xb = XT[m]
        for i in range(2):
            xb = cell(xb, mine + i, m, save=False)
        XO[m] = xb

    def first_row(m, carry):
        @pl.when(xl == 0)
        def _():
            own_stream(m)
            to_left(m).start()
            partner_stream(m)
            to_right(m).start()

        @pl.when(xl == 1)
        def _():
            to_left(m).wait_recv()
            partner_stream(m)
            to_up_right(m).start()
            to_right(m).wait_recv()
            own_stream(m)
            to_up(m).start()

        return carry

    def again(m, carry):
        X[other + 1, m] = cell(X[other, m], other, m)
        cell(X[other + 1, m], other + 1, m, finish=False)
        return carry

    def forward(m, carry):
        f_send(m).wait_recv()
        for j in range(4):
            for i in range(2):
                @pl.when((m == 0) & (y == 1) & (xl != j // 2))
                def _():
                    fw(2 * (j % 2) + i).wait_recv()

            X[j + 1, m] = cell(X[j, m], j, m)

        f_send(m).start()
        return carry

    def b_send(m):
        return rc(GY.at[0, 0, m], GY.at[4, 0, m], b_s.at[m], b_r.at[m], down)

    def nh_send(i, io):
        ref, j = (N, H)[io], 2 * i + 1 - c
        return rc(ref.at[j, 0], ref.at[j, 1], n_s.at[i, io], n_r.at[i, io], sib)

    def e_send(i, io, m):
        ref, j = (GP, GY)[io], 2 * i + 1 - c + io
        return rc(ref.at[j, 0, m], ref.at[j, 1, m], e_s.at[i, io, m], e_r.at[i, io, m], sib)

    def cells_back(ms, mlist):
        for j in range(3, -1, -1):
            gy = flat(GY[j + 1, 0, ms])
            gp = (dot(gy, WOT[j]) * flat(D[j, ms])).astype(bf16)
            put_own(GP, j, ms, gp)
            q = jnp.sum(gp.astype(f32) * flat(PRE[j, ms]), axis=-1, keepdims=True) * (1.0 / C)
            gn = dot(gp, WIT[j])
            r = flat(RS[j, ms])[:, :1]
            n = flat(N[j, 0, ms]).astype(f32)
            put_own(GY, j, ms, (gy.astype(f32) + r * (gn - n * q)).astype(bf16))

            @pl.when(c != j % 2)
            def _():
                for m in mlist:
                    e_send(j // 2, 0, m).start()
                    e_send(j // 2, 1, m).start()

    def backward(m, carry):
        b_send(m).wait_recv()
        cells_back(m, [m])

        @pl.when(y > 0)
        def _():
            b_send(m).start()

        return carry

    def last_row(g, carry):
        mlist = [g * BATCH + i for i in range(BATCH)]
        ms = pl.ds(g * BATCH, BATCH)
        for m in mlist:
            f_send(m).wait_recv()
        xb = flat(X[0, ms])
        for j in range(4):
            xb = cell(xb, j, ms, finish=j < 3)
        cells_back(ms, mlist)
        for m in mlist:
            b_send(m).start()
        return carry

    @pl.when((y > 0) | (xl == 1))
    def _():
        ag_start()

    load_w(0).wait()
    load_w(1).wait()

    @pl.when(y == 0)
    def _():
        @pl.when(xl == 1)
        def _():
            pl.semaphore_wait(diag, 1)

        @pl.when(xl == 0)
        def _():
            for i in range(UNITS):
                load_img(i).wait()
                load_partner_img(i).wait()

        lax.fori_loop(0, M, first_row, 0)

        @pl.when(xl == 0)
        def _():
            ag_start()

        ag_forward()
        fw_wait()

        @pl.when(xl == 1)
        def _():
            for i in range(UNITS):
                load_img(i).wait()

        lax.fori_loop(0, M, again, 0)

    @pl.when(y > 0)
    def _():
        ag_forward()

        @pl.when(y > 1)
        def _():
            fw_wait()
            transpose_weights()

        @pl.when(y < 3)
        def _():
            lax.fori_loop(0, M, forward, 0)

        @pl.when(y == 3)
        def _():
            for i in range(UNITS):
                load_og(i).wait()
            lax.fori_loop(0, M // BATCH, last_row, 0)

    @pl.when(y < 2)
    def _():
        transpose_weights()

    for i in range(2):
        for io in range(2):
            nh_send(i, io).start()
    pl.semaphore_wait(near_z.at[0], 2)
    z_round(1)

    @pl.when(y < 3)
    def _():
        lax.fori_loop(0, 1, backward, 0)

    pl.semaphore_wait(near_z.at[1], 2)
    z_round(2)

    @pl.when(y < 3)
    def _():
        lax.fori_loop(1, 2, backward, 0)

    pl.semaphore_wait(near_z.at[2], 2)
    z_round(3)

    @pl.when(y < 3)
    def _():
        lax.fori_loop(2, M, backward, 0)

    def weight(i, io):
        j = 2 * i + c
        for arr in (0, 1) if io == 1 else ():
            nh_send(i, arr).wait_recv()
            for m in range(M):
                e_send(i, arr, m).wait_recv()
        a, b = ((N.at[j], GP.at[j]), (H.at[j], GY.at[j + 1]))[io]
        g = dot_at(a[...].reshape(2 * OWN, C), b[...].reshape(2 * OWN, C))
        G[i, io] = g.astype(bf16).reshape(2, 8, 2, 16, C)

    xh_r, xh_l = ((x + 1) % 4) // 2, ((x + 3) % 4) // 2
    core = (c, 1 - c)

    def l1(io, e, side):
        return rc(
            G.at[xl, io, 1 - xh, pl.ds(side * 4, 4), core[e]], L1.at[io, e, side],
            p_s.at[io, e, side], p_r.at[io, e, side], (right, left)[side],
        )

    def l2(io, e, side, half):
        rows = pl.ds(half * 4, 4)
        return rc(
            G.at[1 - xl, io, (xh_r, xh_l)[side], rows, core[e]], L2.at[io, e, side, rows],
            q_s.at[io, e, side, half], q_r.at[io, e, side, half], (right, left)[side],
        )

    def first_sends(i, io, e):
        @pl.when(xl == i)
        def _():
            l1(io, e, 0).start()
            l1(io, e, 1).start()

        @pl.when(xl != i)
        def _():
            l2(io, e, 0, 1).start()
            l2(io, e, 1, 0).start()

    def relay(io, e):
        for side, xd in ((0, xh_r), (1, xh_l)):
            l1(io, e, side).wait_recv()
            rows = pl.ds(side * 4, 4)
            G[1 - xl, io, xd, rows, core[e]] = (
                G[1 - xl, io, xd, rows, core[e]].astype(f32) + L1[io, e, side].astype(f32)
            ).astype(bf16)
            l2(io, e, side, side).start()

    def z_send(io, e, off):
        return rc(
            T.at[io, e, (z + off) % 8], LZ.at[io, e, off],
            z_s.at[io, e, off], z_r.at[io, e, off], dev(x, y, (z + off) % 8, core[e]),
        )

    offs = ((4, 3, 5, 2, 6, 1, 7), (4, 3, 5, 2, 6, 1, 7, 0))

    def collect(io, e):
        for side in range(2):
            for half in range(2):
                l2(io, e, side, half).wait_recv()
        T[io, e] = (
            G[xl, io, xh, :, core[e]].astype(f32) + L2[io, e, 0].astype(f32) + L2[io, e, 1].astype(f32)
        ).astype(bf16)
        for off in offs[e]:
            z_send(io, e, off).start()

    def part(chunk):
        return (slice(None), 1, slice(None), chunk, c)

    def zp(n):
        return rc(G.at[part((z + 4 - n) % 8)], ZP.at[n], zp_s.at[n], zp_r.at[n], ring_z(1))

    def zm(n):
        return rc(G.at[part((z + 5 + n) % 8)], ZM.at[n], zm_s.at[n], zm_r.at[n], ring_z(7))

    def ring_step(n):
        zp(n).wait_recv()
        here = part((z + 3 - n) % 8)
        G[here] = (G[here].astype(f32) + ZP[n].astype(f32)).astype(bf16)
        zp(n + 1).start()
        if n < 2:
            zm(n).wait_recv()
            here = part((z + 6 + n) % 8)
            G[here] = (G[here].astype(f32) + ZM[n].astype(f32)).astype(bf16)
            zm(n + 1).start()

    def lx(off):
        to = (x + off) % 4
        return rc(Q.at[to % 2, to // 2], LX.at[off - 1], lx_s.at[off - 1], lx_r.at[off - 1], dev(to, y, z, c))

    weight(1, 1)
    first_sends(1, 1, 1)
    weight(0, 1)
    zp(0).start()
    zm(0).start()
    first_sends(0, 1, 1)
    weight(1, 0)
    first_sends(1, 0, 0)
    weight(0, 0)
    first_sends(0, 0, 0)
    relay(1, 1)
    first_sends(1, 0, 1)
    first_sends(0, 0, 1)
    ring_step(0)
    pl.semaphore_wait(near_z.at[3], 2)
    relay(0, 0)
    collect(1, 1)
    ring_step(1)
    relay(0, 1)
    collect(0, 0)
    ring_step(2)
    collect(0, 1)
    zp(3).wait_recv()
    zm(2).wait_recv()
    Q[...] = (G[part(z)].astype(f32) + ZP[3].astype(f32) + ZM[2].astype(f32)).astype(bf16)
    for off in (2, 1, 3):
        lx(off).start()

    for io, e in ((1, 1), (0, 0), (0, 1)):
        total = T[io, 0, z].astype(f32) if e == 0 else 0.0
        for off in offs[e]:
            z_send(io, e, off).wait_recv()
            total = total + LZ[io, e, off].astype(f32)
        out[io, core[e]] = total
    total = Q[xl, xh].astype(f32)
    for off in range(1, 4):
        lx(off).wait_recv()
        total = total + LX[off - 1].astype(f32)
    out[1, c] = total

    for t in range(4):
        for side in range(2):
            ag(t, side).wait_send()
        fw(t).wait_send()
    for t in SHARED:
        for side in range(2):
            zf(t, side).wait_send()

    @pl.when(y == 0)
    def _():
        for m in range(M):
            to_left(m).wait_send()
            to_right(m).wait_send()

    @pl.when((y > 0) & (y < 3))
    def _():
        for m in range(M):
            f_send(m).wait_send()

    @pl.when(y > 0)
    def _():
        for m in range(M):
            b_send(m).wait_send()

    for io in range(2):
        for i in range(2):
            nh_send(i, io).wait_send()
            for m in range(M):
                e_send(i, io, m).wait_send()
    for io, e in ((1, 1), (0, 0), (0, 1)):
        for side in range(2):
            l1(io, e, side).wait_send()
            for half in range(2):
                l2(io, e, side, half).wait_send()
        for off in offs[e]:
            z_send(io, e, off).wait_send()
    for n in range(4):
        zp(n).wait_send()
    for n in range(3):
        zm(n).wait_send()
        lx(n + 1).wait_send()


def local(images, out_grad, w_in, w_out):
    V = pltpu.VMEM
    REG = pltpu.SemaphoreType.REGULAR
    weights = V((4, C, C), bf16)
    acts = V((4, 2, M, R, C), bf16)
    wide = V((4, M, R, C), f32)
    scratch = [
        weights, weights, weights, weights,
        V((5, M, R, C), bf16), V((M, R, C), bf16), V((M, R, C), bf16),
        acts, acts, acts, V((5, 2, M, R, C), bf16), wide, wide, V((4, M, R, 128), f32),
        V((2, 2, 2, 8, 2, 16, C), bf16),
        V((2, 2, 2, 4, 16, C), bf16), V((2, 2, 2, 8, 16, C), bf16), V((2, 2, 8, 16, C), bf16),
        V((2, 2, 8, 16, C), bf16),
        V((4, 2, 2, 16, C), bf16), V((3, 2, 2, 16, C), bf16), V((2, 2, 16, C), bf16), V((3, 16, C), bf16),
        DMA((2,)), DMA((UNITS,)), DMA((UNITS,)), DMA((4, 2)), DMA((4, 2)), DMA((4,)), DMA((4,)), DMA((4, 2)), DMA((4, 2)),
        DMA((M, 2)), DMA((M, 2)), DMA((M,)), DMA((M,)), DMA((M,)), DMA((M,)),
        DMA((2, 2)), DMA((2, 2)), DMA((2, 2, M)), DMA((2, 2, M)),
        DMA((2, 2, 2)), DMA((2, 2, 2)), DMA((2, 2, 2, 2)), DMA((2, 2, 2, 2)), DMA((2, 2, 8)), DMA((2, 2, 8)),
        DMA((4,)), DMA((4,)), DMA((3,)), DMA((3,)), DMA((3,)), DMA((3,)),
        REG((4,)), REG,
    ]
    grads = pl.pallas_call(
        kernel,
        out_shape=jax.ShapeDtypeStruct((2, 2, 16, C), f32),
        in_specs=[pl.BlockSpec(memory_space=pltpu.HBM)] * 4,
        out_specs=pl.BlockSpec(memory_space=pltpu.VMEM),
        scratch_shapes=scratch,
        compiler_params=pltpu.CompilerParams(
            collective_id=0, has_side_effects=True, vmem_limit_bytes=60 * 2**20
        ),
        name="window",
    )(images, out_grad, w_in, w_out)
    return grads[0][None], grads[1][None]


def solution(mesh):
    return jax.shard_map(
        local,
        mesh=mesh,
        in_specs=(
            P(None, "dp", None),
            P(None, "dp", None),
            P("section", None, None, None),
            P("section", None, None, None),
        ),
        out_specs=(P("section", None, "dp", None), P("section", None, "dp", None)),
        check_vma=False,
    )
```

```python
import jax
import jax.numpy as jnp
from jax import lax
from jax.experimental import pallas as pl
from jax.experimental.pallas import tpu as pltpu
from jax.sharding import PartitionSpec as P

norm_epsilon = 1e-06
f32, bf16 = jnp.float32, jnp.bfloat16
MESH = pl.DeviceIdType.MESH
C = 512
M = 6
R = 64
BATCH = 2
OWN = M * R
UNIT = 96 if R % 96 == 0 else (48 if R == 48 else 32)
UNITS = OWN // UNIT
SHARED, PLAIN = (1, 2, 3), (0,)
DMA = pltpu.SemaphoreType.DMA


def dot(a, b):
    return jnp.dot(a, b, preferred_element_type=f32)


def dot_at(a, b):
    return lax.dot_general(a, b, (((0,), (0,)), ((), ())), preferred_element_type=f32)


def kernel(
    img, og, wi, wo, out,
    WI, WO, WIT, WOT, X, XT, XO, N, H, GP, GY, D, PRE, RS, G, L1, L2, T, LZ, ZP, ZM, Q, LX,
    loc_w, loc_m, loc_x, ag_s, ag_r, fw_s, fw_r, zf_s, zf_r, g_s, g_r, f_s, f_r, b_s, b_r, n_s, n_r, e_s, e_r, p_s, p_r, q_s, q_r, z_s, z_r,
    zp_s, zp_r, zm_s, zm_r, lx_s, lx_r, near_z, diag,
):
    sec = lax.axis_index("section")
    dp = lax.axis_index("dp")
    y, xl = sec // 2, sec % 2
    xh, z, c = dp // 16, (dp // 2) % 8, dp % 2
    x = xh * 2 + xl

    def dev(x_, y_, z_, c_):
        return (y_ * 2 + x_ % 2, (x_ // 2) * 16 + z_ * 2 + c_)

    right, left = dev((x + 1) % 4, y, z, c), dev((x + 3) % 4, y, z, c)
    up, down = dev(x, (y + 1) % 4, z, c), dev(x, (y + 3) % 4, z, c)
    up_right = dev((x + 1) % 4, (y + 1) % 4, z, c)
    sib = dev(x, y, z, 1 - c)

    def ring_z(off):
        return dev(x, y, (z + off) % 8, c)

    def rc(src, dst, ss, rs, to):
        return pltpu.make_async_remote_copy(
            src_ref=src, dst_ref=dst, send_sem=ss, recv_sem=rs, device_id=to, device_id_type=MESH
        )

    def signal(sem, to):
        pl.semaphore_signal(sem, inc=1, device_id=to, device_id_type=MESH)

    mine, other = 2 * xl, 2 * (1 - xl)

    def load_w(i):
        src, dst = ((wi, WI), (wo, WO))[i]
        return pltpu.make_async_copy(src.at[0], dst.at[pl.ds(mine, 2)], loc_w.at[i])

    def load_rows(i, src, half, dst, sem):
        per = 96 // UNIT
        rows = src.at[i // per, pl.ds(half * 96 + (i % per) * UNIT, UNIT)]
        return pltpu.make_async_copy(rows, dst.at[i * UNIT // R, pl.ds(i * UNIT % R, UNIT)], sem.at[i])

    def load_img(i):
        return load_rows(i, img, xl, X.at[0], loc_m)

    def load_partner_img(i):
        return load_rows(i, img, 1, XT, loc_x)

    def load_og(i):
        return load_rows(i, og, xl, GY.at[4, 0], loc_m)

    load_w(0).start()
    load_w(1).start()

    @pl.when(y == 0)
    def _():
        for i in range(UNITS):
            load_img(i).start()

        @pl.when(xl == 0)
        def _():
            for i in range(UNITS):
                load_partner_img(i).start()

    @pl.when(y == 3)
    def _():
        for i in range(UNITS):
            load_og(i).start()

    bar = pltpu.get_barrier_semaphore()
    peers = [right, left, up, down, sib, ring_z(1), ring_z(7)]
    for to in peers:
        signal(bar, to)
    pl.semaphore_wait(bar, len(peers))

    def z_round(n):
        for off in (1, 7):
            signal(near_z.at[n], ring_z(off))

    z_round(0)

    @pl.when((y == 1) & (xl == 1))
    def _():
        signal(diag, down)

    def ag(t, side):
        src, dst = ((wi, WI), (wo, WO))[t % 2]
        k = t // 2
        if t in SHARED:
            rows = pl.ds(c * 256 + side * 128 + (z % 2) * 64, 64)
        else:
            rows = pl.ds(c * 256 + side * 128, 128)
        return rc(src.at[0, k, rows], dst.at[mine + k, rows], ag_s.at[t, side], ag_r.at[t, side], (right, left)[side])

    def ag_start():
        for t in SHARED + PLAIN:
            for side in range(2):
                ag(t, side).start()

    def zf(t, side):
        here = (WI, WO)[t % 2].at[other + t // 2, pl.ds(c * 256 + side * 128 + (z % 2) * 64, 64)]
        return rc(here, here, zf_s.at[t, side], zf_r.at[t, side], ring_z((1, 7)[side]))

    def fw(t):
        dst = (WI, WO)[t % 2]
        here = dst.at[other + t // 2, pl.ds(c * 256, 256)]
        return rc(here, here, fw_s.at[t], fw_r.at[t], sib)

    def ag_forward():
        for t in SHARED:
            for side in range(2):
                ag(t, side).wait_recv()
                zf(t, side).start()
        for t in PLAIN:
            for side in range(2):
                ag(t, side).wait_recv()
            fw(t).start()
        for t in SHARED:
            for side in range(2):
                zf(t, side).wait_recv()
            fw(t).start()

    def fw_wait():
        for t in range(4):
            fw(t).wait_recv()

    def transpose_weights():
        def one(j, carry):
            WIT[j] = WI[j].T
            WOT[j] = WO[j].T
            return carry

        lax.fori_loop(0, 4, one, 0)

    def put(ref, j, ms, value):
        if isinstance(ms, pl.Slice):
            value = value.reshape(ms.size, R, value.shape[-1])
        ref[j, ms] = value

    def put_own(ref, j, ms, value):
        if isinstance(ms, pl.Slice):
            value = value.reshape(ms.size, R, value.shape[-1])
        ref[j, 0, ms] = value

    def flat(value):
        return value.reshape(-1, value.shape[-1])

    def cell(xb, j, ms, save=True, finish=True):
        wide = xb.astype(f32)
        r = lax.rsqrt(jnp.mean(wide * wide, axis=-1, keepdims=True) + norm_epsilon)
        p = dot(xb, WI[j]) * r
        s = 0.5 * jnp.tanh(0.5 * p) + 0.5
        h = p * s
        hb = h.astype(bf16)
        if save:
            put(RS, j, ms, jnp.broadcast_to(r, (r.shape[0], 128)))
            put_own(N, j, ms, (wide * r).astype(bf16))
            put(PRE, j, ms, p)
            put(D, j, ms, s + h * (1.0 - s))
            put_own(H, j, ms, hb)
        if finish:
            return (wide + dot(hb, WO[j])).astype(bf16)

    def f_send(m):
        return rc(X.at[4, m], X.at[0, m], f_s.at[m], f_r.at[m], up)

    def to_left(m):
        return rc(X.at[2, m], XT.at[m], g_s.at[m, 0], g_r.at[m, 1], left)

    def to_right(m):
        return rc(XO.at[m], X.at[2, m], g_s.at[m, 1], g_r.at[m, 0], right)

    def to_up(m):
        return rc(X.at[4, m], X.at[0, m], g_s.at[m, 0], f_r.at[m], up)

    def to_up_right(m):
        return rc(XO.at[m], X.at[0, m], g_s.at[m, 1], f_r.at[m], up_right)

    def own_stream(m):
        xb = X[mine, m]
        for i in range(2):
            xb = cell(xb, mine + i, m)
            X[mine + i + 1, m] = xb

    def partner_stream(m):
        xb = XT[m]
        for i in range(2):
            xb = cell(xb, mine + i, m, save=False)
        XO[m] = xb

    def first_row(m, carry):
        @pl.when(xl == 0)
        def _():
            own_stream(m)
            to_left(m).start()
            partner_stream(m)
            to_right(m).start()

        @pl.when(xl == 1)
        def _():
            to_left(m).wait_recv()
            partner_stream(m)
            to_up_right(m).start()
            to_right(m).wait_recv()
            own_stream(m)
            to_up(m).start()

        return carry

    def again(m, carry):
        X[other + 1, m] = cell(X[other, m], other, m)
        cell(X[other + 1, m], other + 1, m, finish=False)
        return carry

    def forward(m, carry):
        f_send(m).wait_recv()
        for j in range(4):
            for i in range(2):
                @pl.when((m == 0) & (y == 1) & (xl != j // 2))
                def _():
                    fw(2 * (j % 2) + i).wait_recv()

            X[j + 1, m] = cell(X[j, m], j, m)

        f_send(m).start()
        return carry

    def b_send(m):
        return rc(GY.at[0, 0, m], GY.at[4, 0, m], b_s.at[m], b_r.at[m], down)

    def nh_send(i, io):
        ref, j = (N, H)[io], 2 * i + 1 - c
        return rc(ref.at[j, 0], ref.at[j, 1], n_s.at[i, io], n_r.at[i, io], sib)

    def e_send(i, io, m):
        ref, j = (GP, GY)[io], 2 * i + 1 - c + io
        return rc(ref.at[j, 0, m], ref.at[j, 1, m], e_s.at[i, io, m], e_r.at[i, io, m], sib)

    def cells_back(ms, mlist):
        for j in range(3, -1, -1):
            gy = flat(GY[j + 1, 0, ms])
            gp = (dot(gy, WOT[j]) * flat(D[j, ms])).astype(bf16)
            put_own(GP, j, ms, gp)
            q = jnp.sum(gp.astype(f32) * flat(PRE[j, ms]), axis=-1, keepdims=True) * (1.0 / C)
            gn = dot(gp, WIT[j])
            r = flat(RS[j, ms])[:, :1]
            n = flat(N[j, 0, ms]).astype(f32)
            put_own(GY, j, ms, (gy.astype(f32) + r * (gn - n * q)).astype(bf16))

            @pl.when(c != j % 2)
            def _():
                for m in mlist:
                    e_send(j // 2, 0, m).start()
                    e_send(j // 2, 1, m).start()

    def backward(m, carry):
        b_send(m).wait_recv()
        cells_back(m, [m])

        @pl.when(y > 0)
        def _():
            b_send(m).start()

        return carry

    def last_row(g, carry):
        mlist = [g * BATCH + i for i in range(BATCH)]
        ms = pl.ds(g * BATCH, BATCH)
        for m in mlist:
            f_send(m).wait_recv()
        xb = flat(X[0, ms])
        for j in range(4):
            xb = cell(xb, j, ms, finish=j < 3)
        cells_back(ms, mlist)
        for m in mlist:
            b_send(m).start()
        return carry

    @pl.when((y > 0) | (xl == 1))
    def _():
        ag_start()

    load_w(0).wait()
    load_w(1).wait()

    @pl.when(y == 0)
    def _():
        @pl.when(xl == 1)
        def _():
            pl.semaphore_wait(diag, 1)

        @pl.when(xl == 0)
        def _():
            for i in range(UNITS):
                load_img(i).wait()
                load_partner_img(i).wait()

        lax.fori_loop(0, M, first_row, 0)

        @pl.when(xl == 0)
        def _():
            ag_start()

        ag_forward()
        fw_wait()

        @pl.when(xl == 1)
        def _():
            for i in range(UNITS):
                load_img(i).wait()

        lax.fori_loop(0, M, again, 0)

    @pl.when(y > 0)
    def _():
        ag_forward()

        @pl.when(y > 1)
        def _():
            fw_wait()
            transpose_weights()

        @pl.when(y < 3)
        def _():
            lax.fori_loop(0, M, forward, 0)

        @pl.when(y == 3)
        def _():
            for i in range(UNITS):
                load_og(i).wait()
            lax.fori_loop(0, M // BATCH, last_row, 0)

    @pl.when(y < 2)
    def _():
        transpose_weights()

    for i in range(2):
        for io in range(2):
            nh_send(i, io).start()
    pl.semaphore_wait(near_z.at[0], 2)
    z_round(1)

    @pl.when(y < 3)
    def _():
        lax.fori_loop(0, 1, backward, 0)

    pl.semaphore_wait(near_z.at[1], 2)
    z_round(2)

    @pl.when(y < 3)
    def _():
        lax.fori_loop(1, 2, backward, 0)

    pl.semaphore_wait(near_z.at[2], 2)
    z_round(3)

    @pl.when(y < 3)
    def _():
        lax.fori_loop(2, M, backward, 0)

    def weight(i, io):
        j = 2 * i + c
        for arr in (0, 1) if io == 1 else ():
            nh_send(i, arr).wait_recv()
            for m in range(M):
                e_send(i, arr, m).wait_recv()
        a, b = ((N.at[j], GP.at[j]), (H.at[j], GY.at[j + 1]))[io]
        g = dot_at(a[...].reshape(2 * OWN, C), b[...].reshape(2 * OWN, C))
        G[i, io] = g.astype(bf16).reshape(2, 8, 2, 16, C)

    xh_r, xh_l = ((x + 1) % 4) // 2, ((x + 3) % 4) // 2
    core = (c, 1 - c)

    def l1(io, e, side):
        return rc(
            G.at[xl, io, 1 - xh, pl.ds(side * 4, 4), core[e]], L1.at[io, e, side],
            p_s.at[io, e, side], p_r.at[io, e, side], (right, left)[side],
        )

    def l2(io, e, side, half):
        rows = pl.ds(half * 4, 4)
        return rc(
            G.at[1 - xl, io, (xh_r, xh_l)[side], rows, core[e]], L2.at[io, e, side, rows],
            q_s.at[io, e, side, half], q_r.at[io, e, side, half], (right, left)[side],
        )

    def first_sends(i, io, e):
        @pl.when(xl == i)
        def _():
            l1(io, e, 0).start()
            l1(io, e, 1).start()

        @pl.when(xl != i)
        def _():
            l2(io, e, 0, 1).start()
            l2(io, e, 1, 0).start()

    def relay(io, e):
        for side, xd in ((0, xh_r), (1, xh_l)):
            l1(io, e, side).wait_recv()
            rows = pl.ds(side * 4, 4)
            G[1 - xl, io, xd, rows, core[e]] = (
                G[1 - xl, io, xd, rows, core[e]].astype(f32) + L1[io, e, side].astype(f32)
            ).astype(bf16)
            l2(io, e, side, side).start()

    def z_send(io, e, off):
        return rc(
            T.at[io, e, (z + off) % 8], LZ.at[io, e, off],
            z_s.at[io, e, off], z_r.at[io, e, off], dev(x, y, (z + off) % 8, core[e]),
        )

    offs = ((4, 3, 5, 2, 6, 1, 7), (4, 3, 5, 2, 6, 1, 7, 0))

    def collect(io, e):
        for side in range(2):
            for half in range(2):
                l2(io, e, side, half).wait_recv()
        T[io, e] = (
            G[xl, io, xh, :, core[e]].astype(f32) + L2[io, e, 0].astype(f32) + L2[io, e, 1].astype(f32)
        ).astype(bf16)
        for off in offs[e]:
            z_send(io, e, off).start()

    def part(chunk):
        return (slice(None), 1, slice(None), chunk, c)

    def zp(n):
        return rc(G.at[part((z + 4 - n) % 8)], ZP.at[n], zp_s.at[n], zp_r.at[n], ring_z(1))

    def zm(n):
        return rc(G.at[part((z + 5 + n) % 8)], ZM.at[n], zm_s.at[n], zm_r.at[n], ring_z(7))

    def ring_step(n):
        zp(n).wait_recv()
        here = part((z + 3 - n) % 8)
        G[here] = (G[here].astype(f32) + ZP[n].astype(f32)).astype(bf16)
        zp(n + 1).start()
        if n < 2:
            zm(n).wait_recv()
            here = part((z + 6 + n) % 8)
            G[here] = (G[here].astype(f32) + ZM[n].astype(f32)).astype(bf16)
            zm(n + 1).start()

    def lx(off):
        to = (x + off) % 4
        return rc(Q.at[to % 2, to // 2], LX.at[off - 1], lx_s.at[off - 1], lx_r.at[off - 1], dev(to, y, z, c))

    weight(1, 1)
    first_sends(1, 1, 1)
    weight(0, 1)
    zp(0).start()
    zm(0).start()
    first_sends(0, 1, 1)
    weight(1, 0)
    first_sends(1, 0, 0)
    weight(0, 0)
    first_sends(0, 0, 0)
    relay(1, 1)
    first_sends(1, 0, 1)
    first_sends(0, 0, 1)
    ring_step(0)
    pl.semaphore_wait(near_z.at[3], 2)
    relay(0, 0)
    collect(1, 1)
    ring_step(1)
    relay(0, 1)
    collect(0, 0)
    ring_step(2)
    collect(0, 1)
    zp(3).wait_recv()
    zm(2).wait_recv()
    Q[...] = (G[part(z)].astype(f32) + ZP[3].astype(f32) + ZM[2].astype(f32)).astype(bf16)
    for off in (2, 1, 3):
        lx(off).start()

    for io, e in ((1, 1), (0, 0), (0, 1)):
        total = T[io, 0, z].astype(f32) if e == 0 else 0.0
        for off in offs[e]:
            z_send(io, e, off).wait_recv()
            total = total + LZ[io, e, off].astype(f32)
        out[io, core[e]] = total
    total = Q[xl, xh].astype(f32)
    for off in range(1, 4):
        lx(off).wait_recv()
        total = total + LX[off - 1].astype(f32)
    out[1, c] = total

    for t in range(4):
        for side in range(2):
            ag(t, side).wait_send()
        fw(t).wait_send()
    for t in SHARED:
        for side in range(2):
            zf(t, side).wait_send()

    @pl.when(y == 0)
    def _():
        for m in range(M):
            to_left(m).wait_send()
            to_right(m).wait_send()

    @pl.when((y > 0) & (y < 3))
    def _():
        for m in range(M):
            f_send(m).wait_send()

    @pl.when(y > 0)
    def _():
        for m in range(M):
            b_send(m).wait_send()

    for io in range(2):
        for i in range(2):
            nh_send(i, io).wait_send()
            for m in range(M):
                e_send(i, io, m).wait_send()
    for io, e in ((1, 1), (0, 0), (0, 1)):
        for side in range(2):
            l1(io, e, side).wait_send()
            for half in range(2):
                l2(io, e, side, half).wait_send()
        for off in offs[e]:
            z_send(io, e, off).wait_send()
    for n in range(4):
        zp(n).wait_send()
    for n in range(3):
        zm(n).wait_send()
        lx(n + 1).wait_send()


def local(images, out_grad, w_in, w_out):
    V = pltpu.VMEM
    REG = pltpu.SemaphoreType.REGULAR
    weights = V((4, C, C), bf16)
    acts = V((4, 2, M, R, C), bf16)
    wide = V((4, M, R, C), f32)
    scratch = [
        weights, weights, weights, weights,
        V((5, M, R, C), bf16), V((M, R, C), bf16), V((M, R, C), bf16),
        acts, acts, acts, V((5, 2, M, R, C), bf16), wide, wide, V((4, M, R, 128), f32),
        V((2, 2, 2, 8, 2, 16, C), bf16),
        V((2, 2, 2, 4, 16, C), bf16), V((2, 2, 2, 8, 16, C), bf16), V((2, 2, 8, 16, C), bf16),
        V((2, 2, 8, 16, C), bf16),
        V((4, 2, 2, 16, C), bf16), V((3, 2, 2, 16, C), bf16), V((2, 2, 16, C), bf16), V((3, 16, C), bf16),
        DMA((2,)), DMA((UNITS,)), DMA((UNITS,)), DMA((4, 2)), DMA((4, 2)), DMA((4,)), DMA((4,)), DMA((4, 2)), DMA((4, 2)),
        DMA((M, 2)), DMA((M, 2)), DMA((M,)), DMA((M,)), DMA((M,)), DMA((M,)),
        DMA((2, 2)), DMA((2, 2)), DMA((2, 2, M)), DMA((2, 2, M)),
        DMA((2, 2, 2)), DMA((2, 2, 2)), DMA((2, 2, 2, 2)), DMA((2, 2, 2, 2)), DMA((2, 2, 8)), DMA((2, 2, 8)),
        DMA((4,)), DMA((4,)), DMA((3,)), DMA((3,)), DMA((3,)), DMA((3,)),
        REG((4,)), REG,
    ]
    grads = pl.pallas_call(
        kernel,
        out_shape=jax.ShapeDtypeStruct((2, 2, 16, C), f32),
        in_specs=[pl.BlockSpec(memory_space=pltpu.HBM)] * 4,
        out_specs=pl.BlockSpec(memory_space=pltpu.VMEM),
        scratch_shapes=scratch,
        compiler_params=pltpu.CompilerParams(
            collective_id=0, has_side_effects=True, vmem_limit_bytes=60 * 2**20
        ),
        name="window",
    )(images, out_grad, w_in, w_out)
    return grads[0][None], grads[1][None]


def solution(mesh):
    return jax.shard_map(
        local,
        mesh=mesh,
        in_specs=(
            P(None, "dp", None),
            P(None, "dp", None),
            P("section", None, None, None),
            P("section", None, None, None),
        ),
        out_specs=(P("section", None, "dp", None), P("section", None, "dp", None)),
        check_vma=False,
    )
```
